32 devices in a mesh: group: 4 (over z), replica: 8 (over y, x, core).
Axes of the slice: x: 2, y: 2, z: 4, core: 2. Of those that a mesh axis runs over, the one named last changes fastest.
Arguments:
- inputs: bfloat16 [8, 512, 1024], P('replica', 'group'), may hold values from -6 to 6
- cotangent: bfloat16 [8, 512, 1024], P('replica', 'group'), may hold values from -6 to 6
- norm_gain: bfloat16 [2, 2, 1024], P(None, None, 'group'), may hold values from 0.5 to 1.5
- norm_bias: bfloat16 [2, 2, 1024], P(None, None, 'group'), may hold values from -4 to 4
- w_qkv: bfloat16 [2, 1024, 3072], P(None, 'group'), may hold values from -0.1875 to 0.1875
- bias_qv: bfloat16 [2, 2048], P(None, 'group'), may hold values from -6 to 6
- w_out: bfloat16 [2, 1024, 1024], P(None, 'group'), may hold values from -0.75 to 0.75
- bias_out: bfloat16 [2, 1024], P(None, 'group'), may hold values from -6 to 6
- w_up: bfloat16 [2, 1024, 4096], P(None, 'group'), may hold values from -0.1875 to 0.1875
- bias_up: bfloat16 [2, 4096], P(None, 'group'), may hold values from -6 to 6
- w_down: bfloat16 [2, 4096, 1024], P(None, 'group'), may hold values from -0.09375 to 0.09375
- bias_down: bfloat16 [2, 1024], P(None, 'group'), may hold values from -6 to 6
Outputs:
- outputs: bfloat16 [8, 512, 1024], P('replica', 'group')
- input_grad: float32 [8, 512, 1024], P('replica', 'group')
- grad_norm_gain: float32 [2, 2, 1024], P(None, None, 'group')
- grad_norm_bias: float32 [2, 2, 1024], P(None, None, 'group')
- grad_qkv: float32 [2, 1024, 3072], P(None, 'group')
- grad_qv_bias: float32 [2, 2048], P(None, 'group')
- grad_out: float32 [2, 1024, 1024], P(None, 'group')
- grad_out_bias: float32 [2, 1024], P(None, 'group')
- grad_up: float32 [2, 1024, 4096], P(None, 'group')
- grad_up_bias: float32 [2, 4096], P(None, 'group')
- grad_down: float32 [2, 4096, 1024], P(None, 'group')
- grad_down_bias: float32 [2, 1024], P(None, 'group')
The draws below stay inside these ranges and needn't reach their ends.
All inputs are finite; a program needn't handle non-finite values.
Results may differ from the reference program's by a relative error of at most 0.024.
Values may be sent and summed in bfloat16 or wider, within the bound.
A program may use at most 256 MiB of HBM per device.

```python
import jax
import jax.numpy as jnp
from jax import lax

D = 1024
HEADS = 16
HEAD_DIM = 64
FF = 4096
LAYERS = 2
SEQ_LEN = 512
SEQS = 8


def level_of(own_key, extent, pieces, low, high):
    factor_of = 1.0
    for position, shards_of in pieces:
        heights = jax.random.uniform(jax.random.fold_in(jax.random.fold_in(own_key, 6), position), (shards_of,), jnp.float32, low / len(pieces), high / len(pieces))
        factor_of = factor_of * jnp.repeat(jnp.exp(heights), extent[position] // shards_of).reshape((-1,) + (1,) * (len(extent) - 1 - position))
    return factor_of


def noise(key, shape, spread, most, shards=(), kind=jnp.bfloat16):
    factor_of = level_of(key, shape, shards, -0.22, 0.18) if shards else 1.0
    array = jax.random.normal(key, shape, jnp.float32) * spread * factor_of
    return jnp.minimum(jnp.maximum(array, -most), most).astype(kind)


def setup_inputs(seed: int = 0) -> dict:
    splits = jax.random.split(jax.random.key(seed), 13)
    return {
        "inputs": noise(splits[0], (SEQS, SEQ_LEN, D), 1.0, 6.0, ((0, 8), (1, 4))),
        "cotangent": noise(splits[1], (SEQS, SEQ_LEN, D), 1.0, 6.0, ((0, 8), (1, 4))),
        "norm_gain": jnp.clip(1.0 + 0.1 * jax.random.normal(splits[2], (LAYERS, 2, D), jnp.float32), 0.5, 1.5).astype(jnp.bfloat16),
        "norm_bias": noise(splits[3], (LAYERS, 2, D), 0.3, 4.0, ((2, 4),)),
        "w_qkv": noise(splits[4], (LAYERS, D, 3 * D), D ** -0.5, 0.1875, ((1, 4),)),
        "bias_qv": noise(splits[5], (LAYERS, 2 * D), 0.5, 6.0, ((1, 4),)),
        "w_out": noise(splits[6], (LAYERS, D, D), (D // 16) ** -0.5, 0.75, ((1, 4),)),
        "bias_out": noise(splits[7], (LAYERS, D), 0.5, 6.0, ((1, 4),)),
        "w_up": noise(splits[8], (LAYERS, D, FF), D ** -0.5, 0.1875, ((1, 4),)),
        "bias_up": noise(splits[9], (LAYERS, FF), 0.5, 6.0, ((1, 4),)),
        "w_down": noise(splits[10], (LAYERS, FF, D), FF ** -0.5, 0.09375, ((1, 4),)),
        "bias_down": noise(splits[11], (LAYERS, D), 0.5, 6.0, ((1, 4),)),
    }


EPS = 1e-05
NEG = -1e+30
GELU_C = 0.7978845608028654
GELU_A = 0.044715

def head_slopes():
    return 2.0 ** (-8.0 * (jnp.arange(HEADS, dtype=jnp.float32) + 1.0) / HEADS)

def norm_apply(values_in, gain_row, bias_row):
    row_mean = lax.optimization_barrier(jnp.mean(values_in, axis=-1, keepdims=True))
    centered = values_in - row_mean
    variance = lax.optimization_barrier(jnp.mean(centered * centered, axis=-1, keepdims=True))
    inverse = lax.rsqrt(variance + EPS)
    normed = centered * inverse
    return (normed * gain_row + bias_row, normed, inverse)

def norm_back(grad_in, normed, inverse, gain_row):
    scaled = grad_in * gain_row
    return inverse * (scaled - lax.optimization_barrier(jnp.mean(scaled, axis=-1, keepdims=True)) - normed * lax.optimization_barrier(jnp.mean(scaled * normed, axis=-1, keepdims=True)))

def gelu_parts(pre_act):
    tanh_val = jnp.tanh(GELU_C * (pre_act + GELU_A * pre_act * pre_act * pre_act))
    gelu_value = 0.5 * pre_act * (1.0 + tanh_val)
    gelu_slope = 0.5 * (1.0 + tanh_val) + 0.5 * pre_act * (1.0 - tanh_val * tanh_val) * GELU_C * (1.0 + 3.0 * GELU_A * pre_act * pre_act)
    return (gelu_value, gelu_slope)

def split_heads(matrix):
    return matrix.reshape(matrix.shape[0], HEADS, HEAD_DIM)

def attention_scores(queries, keys_all, q_pos, k_pos):
    raw_dots = jnp.einsum('qhd,khd->hqk', queries.astype(jnp.float32), keys_all.astype(jnp.float32))
    offset = (q_pos[:, None] - k_pos[None, :]).astype(jnp.float32)
    scores = raw_dots * HEAD_DIM ** (-0.5) - head_slopes()[:, None, None] * offset[None, :, :]
    return jnp.where((offset >= 0.0)[None, :, :], scores, NEG)

def attend(queries, keys_all, values_all, q_pos, k_pos):
    scores = attention_scores(queries, keys_all, q_pos, k_pos)
    row_top = lax.optimization_barrier(jnp.max(scores, axis=-1, keepdims=True))
    exps_raw = jnp.exp(scores - row_top)
    row_total = lax.optimization_barrier(jnp.sum(exps_raw, axis=-1, keepdims=True))
    log_total = row_top + jnp.log(row_total)
    probs_b16 = jnp.exp(scores - log_total).astype(jnp.bfloat16)
    context = jnp.einsum('hqk,khd->qhd', probs_b16.astype(jnp.float32), values_all.astype(jnp.float32))
    return (context.astype(jnp.bfloat16), log_total)

def attend_back(d_context, context, queries, keys_all, values_all, log_total, q_pos, k_pos):
    scores = attention_scores(queries, keys_all, q_pos, k_pos)
    probs = jnp.exp(scores - log_total)
    probs_b16 = probs.astype(jnp.bfloat16)
    d_probs = jnp.einsum('qhd,khd->hqk', d_context.astype(jnp.float32), values_all.astype(jnp.float32))
    row_delta = lax.optimization_barrier(jnp.sum(d_context.astype(jnp.float32) * context.astype(jnp.float32), axis=-1))
    d_scores = (probs * (d_probs - row_delta.T[:, :, None])).astype(jnp.bfloat16)
    d_query = jnp.einsum('hqk,khd->qhd', d_scores.astype(jnp.float32), keys_all.astype(jnp.float32)) * HEAD_DIM ** (-0.5)
    d_keys = jnp.einsum('hqk,qhd->khd', d_scores.astype(jnp.float32), queries.astype(jnp.float32)) * HEAD_DIM ** (-0.5)
    d_values = jnp.einsum('hqk,qhd->khd', probs_b16.astype(jnp.float32), d_context.astype(jnp.float32))
    return (d_query, d_keys, d_values)

def forward_layer(activation, layer_params, positions):
    norm_g, norm_b, w_qkv, bias_qv, w_out, bias_out, w_up, bias_up, w_down, bias_down = layer_params
    model_width = activation.shape[1]
    normed_in, normed_a, inverse_a = norm_apply(activation, norm_g[0].astype(jnp.float32), norm_b[0].astype(jnp.float32))
    attn_in = normed_in.astype(jnp.bfloat16)
    projected = jnp.dot(attn_in, w_qkv, preferred_element_type=jnp.float32)
    bias_f = bias_qv.astype(jnp.float32)
    queries = split_heads((projected[:, :model_width] + bias_f[:model_width]).astype(jnp.bfloat16))
    keys_all = split_heads(projected[:, model_width:2 * model_width].astype(jnp.bfloat16))
    values_all = split_heads((projected[:, 2 * model_width:] + bias_f[model_width:]).astype(jnp.bfloat16))
    context, log_total = attend(queries, keys_all, values_all, positions, positions)
    context = context.reshape(-1, model_width)
    middle = activation + jnp.dot(context, w_out, preferred_element_type=jnp.float32) + bias_out.astype(jnp.float32)
    mlp_norm, normed_b, inverse_b = norm_apply(middle, norm_g[1].astype(jnp.float32), norm_b[1].astype(jnp.float32))
    mlp_in = mlp_norm.astype(jnp.bfloat16)
    pre_act = jnp.dot(mlp_in, w_up, preferred_element_type=jnp.float32) + bias_up.astype(jnp.float32)
    gelu_value, gelu_slope = gelu_parts(pre_act)
    hidden = gelu_value.astype(jnp.bfloat16)
    result = middle + jnp.dot(hidden, w_down, preferred_element_type=jnp.float32) + bias_down.astype(jnp.float32)
    saved_acts = (normed_a, inverse_a, attn_in, queries, keys_all, values_all, log_total, context, normed_b, inverse_b, mlp_in, gelu_slope, hidden)
    return (result, saved_acts)

def backward_layer(grad_out, layer_params, saved_acts, positions):
    norm_g, norm_b, w_qkv, bias_qv, w_out, bias_out, w_up, bias_up, w_down, bias_down = layer_params
    normed_a, inverse_a, attn_in, queries, keys_all, values_all, log_total, context, normed_b, inverse_b, mlp_in, gelu_slope, hidden = saved_acts
    model_width = grad_out.shape[1]
    grad_b16 = grad_out.astype(jnp.bfloat16)
    g_down = jnp.dot(hidden.T, grad_b16, preferred_element_type=jnp.float32)
    g_down_bias = lax.optimization_barrier(jnp.sum(grad_out, axis=0))
    d_hidden = jnp.dot(grad_b16, w_down.T, preferred_element_type=jnp.float32)
    d_pre = d_hidden * gelu_slope
    g_up_bias = lax.optimization_barrier(jnp.sum(d_pre, axis=0))
    pre_b16 = d_pre.astype(jnp.bfloat16)
    g_up = jnp.dot(mlp_in.T, pre_b16, preferred_element_type=jnp.float32)
    d_mlp_in = jnp.dot(pre_b16, w_up.T, preferred_element_type=jnp.float32)
    g_gain_b = lax.optimization_barrier(jnp.sum(d_mlp_in * normed_b, axis=0))
    g_bias_b = lax.optimization_barrier(jnp.sum(d_mlp_in, axis=0))
    d_resid = grad_out + norm_back(d_mlp_in, normed_b, inverse_b, norm_g[1].astype(jnp.float32))
    resid_b16 = d_resid.astype(jnp.bfloat16)
    g_out = jnp.dot(context.T, resid_b16, preferred_element_type=jnp.float32)
    g_out_bias = lax.optimization_barrier(jnp.sum(d_resid, axis=0))
    d_context = jnp.dot(resid_b16, w_out.T, preferred_element_type=jnp.float32).astype(jnp.bfloat16)
    d_query, d_keys, d_values = attend_back(split_heads(d_context), split_heads(context), queries, keys_all, values_all, log_total, positions, positions)
    d_query = d_query.reshape(-1, model_width)
    d_keys = d_keys.reshape(-1, model_width)
    d_values = d_values.reshape(-1, model_width)
    g_qv_bias = jnp.concatenate([lax.optimization_barrier(jnp.sum(d_query, axis=0)), lax.optimization_barrier(jnp.sum(d_values, axis=0))])
    d_proj = jnp.concatenate([d_query, d_keys, d_values], axis=1).astype(jnp.bfloat16)
    g_qkv = jnp.dot(attn_in.T, d_proj, preferred_element_type=jnp.float32)
    d_attn_in = jnp.dot(d_proj, w_qkv.T, preferred_element_type=jnp.float32)
    g_gain_a = lax.optimization_barrier(jnp.sum(d_attn_in * normed_a, axis=0))
    g_bias_a = lax.optimization_barrier(jnp.sum(d_attn_in, axis=0))
    grad_in = d_resid + norm_back(d_attn_in, normed_a, inverse_a, norm_g[0].astype(jnp.float32))
    layer_grads = (jnp.stack([g_gain_a, g_gain_b]), jnp.stack([g_bias_a, g_bias_b]), g_qkv, g_qv_bias, g_out, g_out_bias, g_up, g_up_bias, g_down, g_down_bias)
    return (grad_in, layer_grads)

def reference(inputs, cotangent, norm_gain, norm_bias, w_qkv, bias_qv, w_out, bias_out, w_up, bias_up, w_down, bias_down):
    params = (norm_gain, norm_bias, w_qkv, bias_qv, w_out, bias_out, w_up, bias_up, w_down, bias_down)
    positions = jnp.arange(SEQ_LEN, dtype=jnp.int32)

    def one_sequence(totals, seq_pair):
        tokens_in, cot_in = seq_pair
        activation = tokens_in.astype(jnp.float32)
        kept_acts = []
        for layer_idx in range(LAYERS):
            layer_params = tuple((member[layer_idx] for member in params))
            activation, saved_acts = forward_layer(activation, layer_params, positions)
            kept_acts.append(saved_acts)
        grad_now = cot_in.astype(jnp.float32)
        per_layer = [None] * LAYERS
        for layer_idx in reversed(range(LAYERS)):
            layer_params = tuple((member[layer_idx] for member in params))
            grad_now, layer_grads = backward_layer(grad_now, layer_params, kept_acts[layer_idx], positions)
            per_layer[layer_idx] = layer_grads
        stacked = tuple((jnp.stack([per_layer[idx_layer][member_idx] for idx_layer in range(LAYERS)]) for member_idx in range(10)))
        new_totals = tuple((total_a + total_b for total_a, total_b in zip(totals, stacked)))
        return (new_totals, (activation.astype(jnp.bfloat16), grad_now))
    init_totals = tuple((jnp.zeros(member.shape, jnp.float32) for member in params))
    totals, (outputs, input_grad) = lax.scan(one_sequence, init_totals, (inputs, cotangent))
    return (outputs, input_grad, totals[0], totals[1], totals[2], totals[3], totals[4], totals[5], totals[6], totals[7], totals[8], totals[9])
```

```python
import functools

import jax
import jax.numpy as jnp
from jax import lax
from jax.experimental import pallas as pl
from jax.experimental.pallas import tpu as pltpu
from jax.sharding import PartitionSpec as P

HEADS = 16
HEAD_DIM = 64

EPS = 1e-05
NEG = -1e30
GELU_C = 0.7978845608028654
GELU_A = 0.044715
F32 = jnp.float32
B16 = jnp.bfloat16
MESH = pl.DeviceIdType.MESH
CH = 2

VMEM = pl.BlockSpec(memory_space=pltpu.VMEM)
ANY = pl.BlockSpec(memory_space=pl.ANY)


def norm_apply(values_in, gain_row, bias_row):
    row_mean = jnp.mean(values_in, axis=-1, keepdims=True)
    centered = values_in - row_mean
    variance = jnp.mean(centered * centered, axis=-1, keepdims=True)
    inverse = lax.rsqrt(variance + EPS)
    normed = centered * inverse
    return (normed * gain_row + bias_row, normed, inverse)


def norm_back(grad_in, normed, inverse, gain_row):
    scaled = grad_in * gain_row
    return inverse * (
        scaled
        - jnp.mean(scaled, axis=-1, keepdims=True)
        - normed * jnp.mean(scaled * normed, axis=-1, keepdims=True)
    )


def gelu_parts(pre_act):
    tanh_val = jnp.tanh(GELU_C * (pre_act + GELU_A * pre_act * pre_act * pre_act))
    gelu_value = 0.5 * pre_act * (1.0 + tanh_val)
    gelu_slope = 0.5 * (1.0 + tanh_val) + 0.5 * pre_act * (1.0 - tanh_val * tanh_val) * GELU_C * (
        1.0 + 3.0 * GELU_A * pre_act * pre_act
    )
    return (gelu_value, gelu_slope)


def dot(a, b):
    return jnp.dot(a, b, preferred_element_type=F32)


def dot_nt(a, b):
    return lax.dot_general(a, b, (((1,), (1,)), ((), ())), preferred_element_type=F32)


def dot_tn(a, b):
    return lax.dot_general(a, b, (((0,), (0,)), ((), ())), preferred_element_type=F32)


def greet_line(n, me):
    barrier = pltpu.get_barrier_semaphore()
    for there, peer in ((me > 0, me - 1), (me < n - 1, me + 1)):

        @pl.when(there)
        def _():
            pl.semaphore_signal(barrier, inc=1, device_id={"group": peer}, device_id_type=MESH)

    beside_me = (me > 0).astype(jnp.int32) + (me < n - 1).astype(jnp.int32)
    pl.semaphore_wait(barrier, beside_me)


def beside(way, me):
    return me + 1 if way == 0 else me - 1


def line_gather(n, me, buf, rows, send_sems, recv_sems, on_block):
    part = rows // CH

    def copy(way, step, chunk, block):
        here = pl.ds(pl.multiple_of(block * rows + chunk * part, part), part)
        return pltpu.make_async_remote_copy(
            src_ref=buf.at[here],
            dst_ref=buf.at[here],
            send_sem=send_sems.at[way, step, chunk],
            recv_sem=recv_sems.at[way, step, chunk],
            device_id={"group": beside(way, me)},
            device_id_type=MESH,
        )

    def block_of(way, step):
        return me - step if way == 0 else me + step

    def have(way, step):
        return me - step >= 0 if way == 0 else me + step < n

    def onward(way):
        return me < n - 1 if way == 0 else me > 0

    for chunk in range(CH):
        for way in (0, 1):

            @pl.when(onward(way))
            def _():
                copy(way, 0, chunk, me).start()

    on_block(me)

    def advance(step, carry):
        for chunk in range(CH):
            for way in (0, 1):

                @pl.when(have(way, step))
                def _():
                    copy(way, step - 1, chunk, block_of(way, step)).wait_recv()

                @pl.when(have(way, step) & onward(way) & (step < n - 1))
                def _():
                    copy(way, step, chunk, block_of(way, step)).start()

        for way in (0, 1):

            @pl.when(have(way, step))
            def _():
                on_block(block_of(way, step))

        return carry

    lax.fori_loop(1, n, advance, 0)

    def drain(step, carry):
        for way in (0, 1):

            @pl.when(have(way, step) & onward(way))
            def _():
                for chunk in range(CH):
                    copy(way, step, chunk, block_of(way, step)).wait_send()

        return carry

    lax.fori_loop(0, n - 1, drain, 0)


def line_scatter(n, me, part, hold, recv, send, final, send_sems, recv_sems):
    def copy(way, step, chunk):
        return pltpu.make_async_remote_copy(
            src_ref=send.at[way, step, chunk],
            dst_ref=recv.at[way, step, chunk],
            send_sem=send_sems.at[way, step, chunk],
            recv_sem=recv_sems.at[way, step, chunk],
            device_id={"group": beside(way, me)},
            device_id_type=MESH,
        )

    def goal(way, step):
        return n - 1 - step if way == 0 else step

    def onward(way, step):
        return goal(way, step) > me if way == 0 else goal(way, step) < me

    def fed(way):
        return me > 0 if way == 0 else me < n - 1

    def advance(step, carry):
        for way in (0, 1):
            on = onward(way, step)

            @pl.when(on)
            def _():
                part(goal(way, step), hold)
                for chunk in range(CH):

                    @pl.when(fed(way))
                    def _():
                        copy(way, step, chunk).wait_recv()
                        send[way, step, chunk] = (hold[chunk] + recv[way, step, chunk].astype(F32)).astype(B16)

                    @pl.when(jnp.logical_not(fed(way)))
                    def _():
                        send[way, step, chunk] = hold[chunk].astype(B16)

                    copy(way, step, chunk).start()

        return carry

    lax.fori_loop(0, n - 1, advance, 0)
    part(me, final)

    def collect(step, carry):
        for way in (0, 1):

            @pl.when((goal(way, step) == me) & fed(way))
            def _():
                for chunk in range(CH):
                    copy(way, step, chunk).wait_recv()
                    final[chunk] = final[chunk] + recv[way, step, chunk].astype(F32)

            @pl.when(onward(way, step))
            def _():
                for chunk in range(CH):
                    copy(way, step, chunk).wait_send()

        return carry

    lax.fori_loop(0, n - 1, collect, 0)


def line_sems(n):
    return [pltpu.SemaphoreType.DMA((2, n - 1, CH)) for _ in range(2)]


def scatter_scratch(n, rows, width):
    cols = width // CH
    return [
        pltpu.VMEM((CH, rows, cols), F32),
        pltpu.VMEM((2, n - 1, CH, rows, cols), B16),
        pltpu.VMEM((2, n - 1, CH, rows, cols), B16),
        pltpu.VMEM((CH, rows, cols), F32),
    ] + line_sems(n)


def rows_at(block, rows):
    return pl.ds(pl.multiple_of(block * rows, rows), rows)


def joined(final):
    return jnp.concatenate([final[chunk] for chunk in range(CH)], axis=1)


def weight_scratch(raw):
    outer, inner, piece, cols = raw.shape
    return [pltpu.VMEM((inner, outer, piece, cols), raw.dtype), pltpu.SemaphoreType.DMA((inner,))]


def weight_copies(raw, held, sems):
    return [
        pltpu.make_async_copy(raw.at[:, i], held.at[i], sems.at[i]) for i in range(held.shape[0])
    ]


def weight_cols(held, lo, size):
    inner, outer, piece, _ = held.shape
    return held[:, :, :, pl.ds(lo, size)].reshape(inner * outer * piece, size)


def weight_rows(held, chunk):
    inner, outer, piece, cols = held.shape
    if inner % CH == 0:
        take = inner // CH
        return held[chunk * take : (chunk + 1) * take].reshape(take * outer * piece, cols)
    take = piece // CH
    return held[0, 0, chunk * take : (chunk + 1) * take, :]


def params(collective_id):
    return pltpu.CompilerParams(
        collective_id=collective_id, has_side_effects=True, vmem_limit_bytes=48 * 1024 * 1024
    )


def cost(us):
    return pl.CostEstimate(flops=0, bytes_accessed=int(us * 3.3e6), transcendentals=0)


STEP_COLS = 256


def forward_kernel(n, layer, mode, *refs):
    refs = list(refs)
    lhs, w_any, res, vec = refs[:4]
    del refs[:4]
    raw = bias = None
    if mode:
        raw, bias = refs[:2]
        del refs[:2]
    after = refs.pop(0)
    y_ref = refs.pop(0)
    outs = []
    if mode:
        count = 3 if mode == "gelu" else 2
        outs = refs[:count]
        del refs[:count]
    w, w_sem, hold, recv, send, final, s_send, s_recv = refs[:8]
    del refs[:8]
    me = lax.axis_index("group")
    rows = res.shape[0]
    w_copy = pltpu.make_async_copy(w_any.at[layer], w, w_sem)
    w_copy.start()
    if mode:
        g_send, g_recv, held, h_sems = refs
        others = weight_copies(raw, held, h_sems)
        for other in others:
            other.start()
    greet_line(n, me)
    w_copy.wait()
    cols = w.shape[1] // CH

    def part(block, into):
        mine = lhs[rows_at(block, rows), :]
        for chunk in range(CH):
            into[chunk] = dot(mine, w[:, chunk * cols : (chunk + 1) * cols])

    line_scatter(n, me, part, hold, recv, send, final, s_send, s_recv)
    y = res[...] + joined(final) + vec[0:1, :]
    y_ref[...] = y
    if not mode:
        return
    all_ref = outs[0]
    all_ref[rows_at(me, rows), :] = norm_apply(y, vec[1:2, :], vec[2:3, :])[0].astype(B16)
    wide = held.shape[-1]
    size = STEP_COLS if wide % STEP_COLS == 0 else wide
    waited = []

    def on_block(block):
        if not waited:
            for other in others:
                other.wait()
            waited.append(True)
        here = rows_at(block, rows)

        def column(i, carry):
            lo = pl.multiple_of(i * size, size)
            value = dot(all_ref[here, :], weight_cols(held, lo, size)) + bias[:, pl.ds(lo, size)]
            if mode == "gelu":
                value, slope = gelu_parts(value)
                outs[2][here, pl.ds(lo, size)] = slope
            outs[1][here, pl.ds(lo, size)] = value.astype(B16)
            return carry

        lax.fori_loop(0, wide // size, column, 0)

    line_gather(n, me, all_ref, rows, g_send, g_recv, on_block)


def forward_step(lhs, w_all, layer, res, vec, collective_id, mode=None, raw=None, bias=None, after=None):
    n = lax.axis_size("group")
    rows, width = res.shape
    depth = w_all.shape[1]
    ins = [lhs, w_all, res, vec]
    specs = [VMEM, ANY, VMEM, VMEM]
    outs = [jax.ShapeDtypeStruct((rows, width), F32)]
    scratch = [pltpu.VMEM((depth, width), B16), pltpu.SemaphoreType.DMA] + scatter_scratch(n, rows, width)
    us = 21.0
    if mode:
        us = 42.0
        ins += [raw, bias]
        specs += [ANY, VMEM]
        wide = raw.shape[-1]
        outs += [
            jax.ShapeDtypeStruct((n * rows, width), B16),
            jax.ShapeDtypeStruct((n * rows, wide), B16),
        ]
        if mode == "gelu":
            outs.append(jax.ShapeDtypeStruct((n * rows, wide), F32))
        scratch += line_sems(n) + weight_scratch(raw)
    ins.append(lhs if after is None else after)
    specs.append(ANY)
    return pl.pallas_call(
        functools.partial(forward_kernel, n, layer, mode),
        out_shape=outs,
        in_specs=specs,
        out_specs=[VMEM] * len(outs),
        scratch_shapes=scratch,
        compiler_params=params(collective_id),
        cost_estimate=cost(us),
        name=f"forward_{mode}_{layer}",
    )(*ins)


def backward_kernel(n, layer, mode, *refs):
    refs = list(refs)
    lhs, raw, xin, gain, res = refs[:5]
    del refs[:5]
    if mode:
        w_any = refs.pop(0)
    if mode == "gelu":
        slope = refs.pop(0)
    after = refs.pop(0)
    g_ref, small_ref = refs[:2]
    del refs[:2]
    if mode:
        all_ref, t_ref = refs[:2]
        del refs[:2]
    if mode == "gelu":
        sum_ref = refs.pop(0)
    held, h_sems, hold, recv, send, final, s_send, s_recv = refs[:8]
    del refs[:8]
    me = lax.axis_index("group")
    rows = res.shape[0]
    others = weight_copies(raw, held, h_sems)
    for other in others:
        other.start()
    if mode:
        g_send, g_recv, w, w_sem = refs
        w_copy = pltpu.make_async_copy(w_any.at[layer], w, w_sem)
        w_copy.start()
    greet_line(n, me)
    for other in others:
        other.wait()

    def part(block, into):
        mine = lhs[rows_at(block, rows), :]
        for chunk in range(CH):
            into[chunk] = dot_nt(mine, weight_rows(held, chunk))

    line_scatter(n, me, part, hold, recv, send, final, s_send, s_recv)
    grad = joined(final)
    _, normed, inverse = norm_apply(xin[...], gain[...], gain[...])
    result = res[...] + norm_back(grad, normed, inverse, gain[...])
    g_ref[...] = result
    small_ref[0:1, :] = jnp.sum(grad * normed, axis=0, keepdims=True)
    small_ref[1:2, :] = jnp.sum(grad, axis=0, keepdims=True)
    small_ref[2:3, :] = jnp.sum(result, axis=0, keepdims=True)
    if not mode:
        return
    all_ref[rows_at(me, rows), :] = result.astype(B16)
    wide = w.shape[0]
    size = STEP_COLS if wide % STEP_COLS == 0 else wide
    if mode == "gelu":
        sum_ref[...] = jnp.zeros_like(sum_ref)
    waited = []

    def on_block(block):
        if not waited:
            w_copy.wait()
            waited.append(True)
        here = rows_at(block, rows)

        def column(i, carry):
            lo = pl.multiple_of(i * size, size)
            value = dot_nt(all_ref[here, :], w[pl.ds(lo, size), :])
            if mode == "gelu":
                value = value * slope[here, pl.ds(lo, size)]
                sum_ref[:, pl.ds(lo, size)] += jnp.sum(value, axis=0, keepdims=True)
            t_ref[here, pl.ds(lo, size)] = value.astype(B16)
            return carry

        lax.fori_loop(0, wide // size, column, 0)

    line_gather(n, me, all_ref, rows, g_send, g_recv, on_block)


def backward_step(lhs, raw, xin, gain, res, collective_id, mode=None, w_all=None, layer=0, slope=None, after=None):
    n = lax.axis_size("group")
    rows, width = res.shape
    ins = [lhs, raw, xin, gain, res]
    specs = [VMEM, ANY, VMEM, VMEM, VMEM]
    outs = [jax.ShapeDtypeStruct((rows, width), F32), jax.ShapeDtypeStruct((8, width), F32)]
    scratch = weight_scratch(raw) + scatter_scratch(n, rows, width)
    us = 21.0
    if mode:
        us = 42.0
        ins.append(w_all)
        specs.append(ANY)
        wide = w_all.shape[1]
        outs += [
            jax.ShapeDtypeStruct((n * rows, width), B16),
            jax.ShapeDtypeStruct((n * rows, wide), B16),
        ]
        scratch += line_sems(n) + [pltpu.VMEM((wide, width), B16), pltpu.SemaphoreType.DMA]
    if mode == "gelu":
        ins.append(slope)
        specs.append(VMEM)
        outs.append(jax.ShapeDtypeStruct((1, wide), F32))
    ins.append(lhs if after is None else after)
    specs.append(ANY)
    return pl.pallas_call(
        functools.partial(backward_kernel, n, layer, mode),
        out_shape=outs,
        in_specs=specs,
        out_specs=[VMEM] * len(outs),
        scratch_shapes=scratch,
        compiler_params=params(collective_id),
        cost_estimate=cost(us),
        name=f"backward_{mode}_{layer}",
    )(*ins)


def first_kernel(n, normed, x_ref, vec, after, all_ref, g_send, g_recv):
    me = lax.axis_index("group")
    rows = x_ref.shape[0]
    greet_line(n, me)
    value = x_ref[...]
    if normed:
        value = norm_apply(value.astype(F32), vec[0:1, :], vec[1:2, :])[0].astype(B16)
    all_ref[rows_at(me, rows), :] = value
    line_gather(n, me, all_ref, rows, g_send, g_recv, lambda block: None)


def first_gather(x, vec, collective_id, normed, after):
    n = lax.axis_size("group")
    rows, width = x.shape
    return pl.pallas_call(
        functools.partial(first_kernel, n, normed),
        out_shape=jax.ShapeDtypeStruct((n * rows, width), B16),
        in_specs=[VMEM, VMEM, ANY],
        out_specs=VMEM,
        scratch_shapes=line_sems(n),
        compiler_params=params(collective_id),
        cost_estimate=cost(21.0),
        name="first_gather" if normed else "cot_gather",
    )(x, vec, after)


def swap_kernel(n, count, *refs):
    ins, outs = refs[:count], refs[count + 1 : 2 * count + 1]
    send_sems, recv_sems, own_sems = refs[2 * count + 1 :]
    me = lax.axis_index("group")
    peers = [lax.rem(me + step, n) for step in range(1, n)]
    barrier = pltpu.get_barrier_semaphore()
    for peer in peers:
        pl.semaphore_signal(barrier, inc=1, device_id={"group": peer}, device_id_type=MESH)
    pl.semaphore_wait(barrier, n - 1)
    copies = []
    for k in range(count):
        for step, peer in enumerate(peers):
            copy = pltpu.make_async_remote_copy(
                src_ref=ins[k].at[peer],
                dst_ref=outs[k].at[me],
                send_sem=send_sems.at[k, step],
                recv_sem=recv_sems.at[k, step],
                device_id={"group": peer},
                device_id_type=MESH,
            )
            copy.start()
            copies.append(copy)
        own = pltpu.make_async_copy(ins[k].at[me], outs[k].at[me], own_sems.at[k])
        own.start()
        copies.append(own)
    for copy in copies:
        copy.wait()


def swap(blocks, collective_id, after=None, us=8.0):
    n = lax.axis_size("group")
    count = len(blocks)
    return pl.pallas_call(
        functools.partial(swap_kernel, n, count),
        out_shape=[jax.ShapeDtypeStruct(b.shape, b.dtype) for b in blocks],
        in_specs=[VMEM] * count + [ANY],
        out_specs=[VMEM] * count,
        scratch_shapes=[pltpu.SemaphoreType.DMA((count, n - 1)) for _ in range(2)]
        + [pltpu.SemaphoreType.DMA((count,))],
        compiler_params=params(collective_id),
        cost_estimate=cost(us),
        name=f"swap_{collective_id}",
    )(*blocks, blocks[0] if after is None else after)


def grads_kernel(n, a_ref, b_ref, c_ref, d_ref, o_ref, held, sems):
    own = held.shape[0]
    cols, width = b_ref.shape[1], d_ref.shape[1]
    folds = c_ref.shape[1] // own
    copies = []
    for i in range(n + folds):
        if i < n:
            lo, size = i * cols, cols
            value = dot_tn(a_ref[:, i * own : (i + 1) * own], b_ref[...])
        else:
            lo, size = n * cols + (i - n) * width, width
            value = dot_tn(c_ref[:, (i - n) * own : (i - n + 1) * own], d_ref[...])
        held[:, lo : lo + size] = value.astype(B16)
        copy = pltpu.make_async_copy(
            held.at[:, pl.ds(lo, size)], o_ref.at[:, pl.ds(lo, size)], sems.at[i]
        )
        copy.start()
        copies.append(copy)
    for copy in copies:
        copy.wait()


def grads_pair(a, b, c, d):
    n = lax.axis_size("group")
    own = a.shape[1] // n
    folds = c.shape[1] // own
    total = n * b.shape[1] + folds * d.shape[1]
    return pl.pallas_call(
        functools.partial(grads_kernel, n),
        out_shape=jax.ShapeDtypeStruct((own, total), B16),
        in_specs=[VMEM] * 4,
        out_specs=ANY,
        scratch_shapes=[pltpu.VMEM((own, total), B16), pltpu.SemaphoreType.DMA((n + folds,))],
        compiler_params=pltpu.CompilerParams(vmem_limit_bytes=32 * 1024 * 1024),
        cost_estimate=cost(4.0),
        name="weight_grads",
    )(a, b, c, d)


def attention(q, k, v, first_head, heads_here):
    tokens = q.shape[0]
    split = lambda m: m.reshape(tokens, heads_here, HEAD_DIM).transpose(1, 0, 2)
    q, k, v = split(q), split(k), split(v)
    head_ids = (first_head + jnp.arange(heads_here, dtype=jnp.int32)).astype(F32)
    slopes = 2.0 ** (-8.0 * (head_ids + 1.0) / HEADS)
    pos = jnp.arange(tokens, dtype=jnp.int32)
    offset = (pos[:, None] - pos[None, :]).astype(F32)
    raw = jnp.einsum("hqd,hkd->hqk", q, k, preferred_element_type=F32)
    scores = raw * HEAD_DIM ** (-0.5) - slopes[:, None, None] * offset[None]
    scores = jnp.where((offset >= 0.0)[None], scores, NEG)
    row_top = jnp.max(scores, axis=-1, keepdims=True)
    exps_raw = jnp.exp(scores - row_top)
    row_total = jnp.sum(exps_raw, axis=-1, keepdims=True)
    probs = (exps_raw * (1.0 / row_total)).astype(B16)
    context = jnp.einsum("hqk,hkd->hqd", probs, v, preferred_element_type=F32).astype(B16)
    return context.transpose(1, 0, 2).reshape(tokens, -1), (q, k, v, probs, context)


def attention_back(d_context, saved):
    q, k, v, probs, context = saved
    heads_here, tokens, _ = q.shape
    dc = d_context.reshape(tokens, heads_here, HEAD_DIM).transpose(1, 0, 2)
    d_probs = jnp.einsum("hqd,hkd->hqk", dc, v, preferred_element_type=F32)
    delta = jnp.sum(dc.astype(F32) * context.astype(F32), axis=-1, keepdims=True)
    ds = (probs.astype(F32) * (d_probs - delta)).astype(B16)
    scale = HEAD_DIM ** (-0.5)
    dq = jnp.einsum("hqk,hkd->hqd", ds, k, preferred_element_type=F32) * scale
    dk = jnp.einsum("hqk,hqd->hkd", ds, q, preferred_element_type=F32) * scale
    dv = jnp.einsum("hqk,hqd->hkd", probs, dc, preferred_element_type=F32)
    sums = (jnp.sum(dq, axis=1).reshape(-1), jnp.sum(dv, axis=1).reshape(-1))
    join = lambda m: m.astype(B16).transpose(1, 0, 2).reshape(tokens, -1)
    return jnp.concatenate([join(dq), join(dk), join(dv)], axis=1), sums


def local(
    inputs,
    cotangent,
    norm_gain,
    norm_bias,
    w_qkv,
    bias_qv,
    w_out,
    bias_out,
    w_up,
    bias_up,
    w_down,
    bias_down,
):
    groups = lax.axis_size("group")
    replicas = lax.axis_size("replica")
    me = lax.axis_index("group")
    copy_idx = lax.axis_index("replica")
    layers, own, _ = w_qkv.shape
    width = own * groups
    ff_own = w_down.shape[1]
    heads_here = HEADS // groups
    piece = own // replicas

    qkv_piece = lax.dynamic_slice_in_dim(w_qkv, copy_idx * piece, piece, axis=1)
    qkv_piece = qkv_piece.reshape(layers, piece, 3, groups, own).transpose(0, 3, 1, 2, 4)
    qkv_piece = qkv_piece.reshape(layers, groups, piece, 3 * own)
    up_piece = lax.dynamic_slice_in_dim(w_up, copy_idx * piece, piece, axis=1)
    up_piece = up_piece.reshape(layers, piece, groups, ff_own).transpose(0, 2, 1, 3)

    def share(block):
        full = lax.all_gather(block, "replica", axis=0)
        if piece % 16:
            full = full.transpose(1, 0, 2, 3).reshape(1, 1, width, -1)
        return full

    small = jnp.concatenate(
        [norm_gain, norm_bias, bias_qv.reshape(layers, 2, own), bias_out[:, None], bias_down[:, None]],
        axis=1,
    ).reshape(layers * 8, own)
    small = jnp.broadcast_to(small[None], (groups,) + small.shape)
    small, wq_first = swap([small, qkv_piece[0]], 0)
    wq = [share(wq_first)] + [None] * (layers - 1)
    wu = [None] * layers

    small = small.reshape(groups, layers, 8, own).astype(F32)
    rows_of = lambda i: small[:, :, i].transpose(1, 0, 2).reshape(layers, width)
    gains = [rows_of(0), rows_of(1)]
    shifts = [rows_of(2), rows_of(3)]
    qv_full = small[:, :, 4:6].transpose(1, 0, 2, 3).reshape(layers, 2 * width)
    q_bias = lax.dynamic_slice_in_dim(qv_full, me * own, own, axis=1)
    v_bias = lax.dynamic_slice_in_dim(qv_full, width + me * own, own, axis=1)
    qkv_bias = jnp.concatenate([q_bias, jnp.zeros_like(q_bias), v_bias], axis=1)
    out_bias, down_bias = rows_of(6), rows_of(7)
    up_bias = bias_up.astype(F32)

    x = inputs[0].astype(F32)
    vec0 = jnp.stack([gains[0][0], shifts[0][0]])
    a1_all = first_gather(inputs[0], vec0, 1, True, wq_first)
    later = [up_piece[l] for l in range(layers)] + [qkv_piece[l] for l in range(1, layers)]
    later = swap(later, 2, a1_all, 24.0)
    for l in range(layers):
        wu[l] = share(later[l])
        if l:
            wq[l] = share(later[layers + l - 1])
    cot_all = first_gather(cotangent[0], vec0, 3, False, later[0])

    full0 = wq[0].transpose(1, 0, 2, 3).reshape(width, 3 * own)
    proj = (dot(a1_all, full0) + qkv_bias[0]).astype(B16)
    kept = []
    for l in range(layers):
        cut = lambda i: proj[:, i * own : (i + 1) * own]
        context, attn_saved = attention(cut(0), cut(1), cut(2), me * heads_here, heads_here)
        vec = jnp.stack([out_bias[l], gains[1][l], shifts[1][l]])
        h, a2_all, hidden, slope = forward_step(
            context, w_out, l, x, vec, 10 + 4 * l, "gelu", wu[l], up_bias[l][None]
        )
        saved = (x, a1_all, attn_saved, context, h, a2_all, slope, hidden)
        if l + 1 < layers:
            vec = jnp.stack([down_bias[l], gains[0][l + 1], shifts[0][l + 1]])
            x, a1_all, proj = forward_step(
                hidden, w_down, l, h, vec, 11 + 4 * l, "bias", wq[l + 1], qkv_bias[l + 1][None]
            )
        else:
            vec = jnp.stack([down_bias[l], down_bias[l], down_bias[l]])
            (x,) = forward_step(hidden, w_down, l, h, vec, 11 + 4 * l)
        kept.append(saved)
    outputs = x.astype(B16)[None]

    def reduce_pair(grads):
        return lax.psum_scatter(grads, "replica", scatter_dimension=0, tiled=True)

    def share_pair(mine, cols, minor, collective_id, after=None):
        cut = groups * cols
        left = mine[:, :cut].reshape(piece, groups, cols).transpose(1, 0, 2)
        (left,) = swap([left], collective_id, after)
        left = left.reshape(groups, piece, minor, cols // minor).transpose(1, 2, 0, 3)
        mine = jnp.concatenate([left.reshape(piece, cut), mine[:, cut:]], axis=1)
        return lax.all_gather(mine, "replica", axis=0, tiled=True)

    def unpack_pair(full, cols):
        cut = groups * cols
        folds = (full.shape[1] - cut) // width
        rows = [full[:, cut + i * width : cut + (i + 1) * width] for i in range(folds)]
        return full[:, :cut].astype(F32), jnp.concatenate(rows, axis=0).astype(F32)

    g = cotangent[0].astype(F32)
    g_sum = jnp.sum(g, axis=0)
    g_all = cot_all
    smalls = [None] * layers
    ffn_sum = [None] * layers
    attn_sum = [None] * layers
    ffn_full = [None] * layers
    attn_full = [None] * layers
    zeros_qv = jnp.zeros((2 * width,), F32)
    pre = up_sum = None
    for l in reversed(range(layers)):
        x_in, a1_all, attn_saved, context, h, a2_all, slope, hidden = kept[l]
        if pre is None:
            d_pre = dot_nt(g_all, w_down[l]) * slope
            up_sum = jnp.sum(d_pre, axis=0)
            pre = d_pre.astype(B16)
        ffn_grads = grads_pair(a2_all, pre, hidden, g_all)
        ffn_sum[l] = reduce_pair(ffn_grads)
        down_sum = g_sum
        dh, small1, dh_all, dc = backward_step(
            pre, wu[l], h, gains[1][l][None], g, 30 + 4 * l, "plain", w_out, l
        )
        d_proj, (dq_sum, dv_sum) = attention_back(dc, attn_saved)
        attn_grads = grads_pair(a1_all, d_proj, context, dh_all)
        attn_sum[l] = reduce_pair(attn_grads)
        ffn_full[l] = share_pair(ffn_sum[l], ff_own, 1, 60 + 4 * l)
        ups = up_sum
        if l:
            below = kept[l - 1]
            g, small0, g_all, pre, up_sum = backward_step(
                d_proj, wq[l], x_in, gains[0][l][None], dh, 31 + 4 * l, "gelu", w_down, l - 1, below[6],
                after=attn_grads,
            )
            g_sum, up_sum = small0[2], up_sum[0]
        else:
            g, small0 = backward_step(
                d_proj, wq[l], x_in, gains[0][l][None], dh, 31 + 4 * l, after=attn_grads
            )
        attn_full[l] = share_pair(attn_sum[l], 3 * own, 3, 61 + 4 * l)
        qv = lax.dynamic_update_slice_in_dim(zeros_qv, dq_sum, me * own, axis=0)
        qv = lax.dynamic_update_slice_in_dim(qv, dv_sum, width + me * own, axis=0)
        smalls[l] = (
            jnp.concatenate([small0[0], small1[0], small0[1], small1[1], qv, small1[2], down_sum]),
            ups,
        )

    grads = [unpack_pair(attn_full[l], 3 * own) + unpack_pair(ffn_full[l], ff_own) for l in range(layers)]

    wide = jnp.stack([s[0] for s in smalls])
    per_owner = lambda lo, n: wide[:, lo * width : (lo + n) * width].reshape(layers, n, groups, own)
    gain_bias = per_owner(0, 4).transpose(2, 0, 1, 3)
    qv = wide[:, 4 * width : 6 * width].reshape(layers, groups, 2, own).transpose(1, 0, 2, 3)
    dense = per_owner(6, 2).transpose(2, 0, 1, 3)
    wide = jnp.concatenate([gain_bias, qv, dense], axis=2)
    (mine,) = swap([wide.reshape(groups, layers * 8, own)], 5)
    mine = jnp.sum(mine, axis=0)
    ups = jnp.stack([s[1] for s in smalls])
    flat = jnp.concatenate([mine.reshape(-1), ups.reshape(-1)]).reshape(-1, 128)
    total = lax.psum(flat, "replica").reshape(-1)
    cut = layers * 8 * own
    own_cols = total[:cut].reshape(layers, 8, own)
    up_total = total[cut:].reshape(layers, ff_own)
    qv_total = own_cols[:, 4:6].reshape(layers, 2 * own)
    stack = lambda i: jnp.stack([grads[l][i] for l in range(layers)])
    return (
        outputs,
        g[None],
        own_cols[:, 0:2],
        own_cols[:, 2:4],
        stack(0),
        qv_total,
        stack(1),
        own_cols[:, 6],
        stack(2),
        up_total,
        stack(3),
        own_cols[:, 7],
    )


def solution(mesh):
    rows = P("replica", "group", None)
    vec = P(None, None, "group")
    mat = P(None, "group", None)
    bias = P(None, "group")
    params_in = (vec, vec, mat, bias, mat, bias, mat, bias, mat, bias)
    return jax.shard_map(
        local,
        mesh=mesh,
        in_specs=(rows, rows) + params_in,
        out_specs=(rows, rows) + params_in,
        check_vma=False,
    )
```

```python
import functools

import jax
import jax.numpy as jnp
from jax import lax
from jax.experimental import pallas as pl
from jax.experimental.pallas import tpu as pltpu
from jax.sharding import PartitionSpec as P

HEADS = 16
HEAD_DIM = 64

EPS = 1e-05
NEG = -1e30
GELU_C = 0.7978845608028654
GELU_A = 0.044715
F32 = jnp.float32
B16 = jnp.bfloat16
MESH = pl.DeviceIdType.MESH
CH = 2

VMEM = pl.BlockSpec(memory_space=pltpu.VMEM)
ANY = pl.BlockSpec(memory_space=pl.ANY)


def norm_apply(values_in, gain_row, bias_row):
    row_mean = jnp.mean(values_in, axis=-1, keepdims=True)
    centered = values_in - row_mean
    variance = jnp.mean(centered * centered, axis=-1, keepdims=True)
    inverse = lax.rsqrt(variance + EPS)
    normed = centered * inverse
    return (normed * gain_row + bias_row, normed, inverse)


def norm_back(grad_in, normed, inverse, gain_row):
    scaled = grad_in * gain_row
    return inverse * (
        scaled
        - jnp.mean(scaled, axis=-1, keepdims=True)
        - normed * jnp.mean(scaled * normed, axis=-1, keepdims=True)
    )


def gelu_parts(pre_act):
    tanh_val = jnp.tanh(GELU_C * (pre_act + GELU_A * pre_act * pre_act * pre_act))
    gelu_value = 0.5 * pre_act * (1.0 + tanh_val)
    gelu_slope = 0.5 * (1.0 + tanh_val) + 0.5 * pre_act * (1.0 - tanh_val * tanh_val) * GELU_C * (
        1.0 + 3.0 * GELU_A * pre_act * pre_act
    )
    return (gelu_value, gelu_slope)


def dot(a, b):
    return jnp.dot(a, b, preferred_element_type=F32)


def dot_nt(a, b):
    return lax.dot_general(a, b, (((1,), (1,)), ((), ())), preferred_element_type=F32)


def dot_tn(a, b):
    return lax.dot_general(a, b, (((0,), (0,)), ((), ())), preferred_element_type=F32)


def greet_line(n, me):
    barrier = pltpu.get_barrier_semaphore()
    for there, peer in ((me > 0, me - 1), (me < n - 1, me + 1)):

        @pl.when(there)
        def _():
            pl.semaphore_signal(barrier, inc=1, device_id={"group": peer}, device_id_type=MESH)

    beside_me = (me > 0).astype(jnp.int32) + (me < n - 1).astype(jnp.int32)
    pl.semaphore_wait(barrier, beside_me)


def beside(way, me):
    return me + 1 if way == 0 else me - 1


def line_gather(n, me, buf, rows, send_sems, recv_sems, on_block):
    part = rows // CH

    def copy(way, step, chunk, block):
        here = pl.ds(pl.multiple_of(block * rows + chunk * part, part), part)
        return pltpu.make_async_remote_copy(
            src_ref=buf.at[here],
            dst_ref=buf.at[here],
            send_sem=send_sems.at[way, step, chunk],
            recv_sem=recv_sems.at[way, step, chunk],
            device_id={"group": beside(way, me)},
            device_id_type=MESH,
        )

    def block_of(way, step):
        return me - step if way == 0 else me + step

    def have(way, step):
        return me - step >= 0 if way == 0 else me + step < n

    def onward(way):
        return me < n - 1 if way == 0 else me > 0

    for chunk in range(CH):
        for way in (0, 1):

            @pl.when(onward(way))
            def _():
                copy(way, 0, chunk, me).start()

    on_block(me)

    def advance(step, carry):
        for chunk in range(CH):
            for way in (0, 1):

                @pl.when(have(way, step))
                def _():
                    copy(way, step - 1, chunk, block_of(way, step)).wait_recv()

                @pl.when(have(way, step) & onward(way) & (step < n - 1))
                def _():
                    copy(way, step, chunk, block_of(way, step)).start()

        for way in (0, 1):

            @pl.when(have(way, step))
            def _():
                on_block(block_of(way, step))

        return carry

    lax.fori_loop(1, n, advance, 0)

    def drain(step, carry):
        for way in (0, 1):

            @pl.when(have(way, step) & onward(way))
            def _():
                for chunk in range(CH):
                    copy(way, step, chunk, block_of(way, step)).wait_send()

        return carry

    lax.fori_loop(0, n - 1, drain, 0)


def line_scatter(n, me, part, hold, recv, send, final, send_sems, recv_sems):
    def copy(way, step, chunk):
        return pltpu.make_async_remote_copy(
            src_ref=send.at[way, step, chunk],
            dst_ref=recv.at[way, step, chunk],
            send_sem=send_sems.at[way, step, chunk],
            recv_sem=recv_sems.at[way, step, chunk],
            device_id={"group": beside(way, me)},
            device_id_type=MESH,
        )

    def goal(way, step):
        return n - 1 - step if way == 0 else step

    def onward(way, step):
        return goal(way, step) > me if way == 0 else goal(way, step) < me

    def fed(way):
        return me > 0 if way == 0 else me < n - 1

    def advance(step, carry):
        for way in (0, 1):
            on = onward(way, step)

            @pl.when(on)
            def _():
                part(goal(way, step), hold)
                for chunk in range(CH):

                    @pl.when(fed(way))
                    def _():
                        copy(way, step, chunk).wait_recv()
                        send[way, step, chunk] = (hold[chunk] + recv[way, step, chunk].astype(F32)).astype(B16)

                    @pl.when(jnp.logical_not(fed(way)))
                    def _():
                        send[way, step, chunk] = hold[chunk].astype(B16)

                    copy(way, step, chunk).start()

        return carry

    lax.fori_loop(0, n - 1, advance, 0)
    part(me, final)

    def collect(step, carry):
        for way in (0, 1):

            @pl.when((goal(way, step) == me) & fed(way))
            def _():
                for chunk in range(CH):
                    copy(way, step, chunk).wait_recv()
                    final[chunk] = final[chunk] + recv[way, step, chunk].astype(F32)

            @pl.when(onward(way, step))
            def _():
                for chunk in range(CH):
                    copy(way, step, chunk).wait_send()

        return carry

    lax.fori_loop(0, n - 1, collect, 0)


def line_sems(n):
    return [pltpu.SemaphoreType.DMA((2, n - 1, CH)) for _ in range(2)]


def scatter_scratch(n, rows, width):
    cols = width // CH
    return [
        pltpu.VMEM((CH, rows, cols), F32),
        pltpu.VMEM((2, n - 1, CH, rows, cols), B16),
        pltpu.VMEM((2, n - 1, CH, rows, cols), B16),
        pltpu.VMEM((CH, rows, cols), F32),
    ] + line_sems(n)


def rows_at(block, rows):
    return pl.ds(pl.multiple_of(block * rows, rows), rows)


def joined(final):
    return jnp.concatenate([final[chunk] for chunk in range(CH)], axis=1)


def weight_scratch(raw):
    outer, inner, piece, cols = raw.shape
    return [pltpu.VMEM((inner, outer, piece, cols), raw.dtype), pltpu.SemaphoreType.DMA((inner,))]


def weight_copies(raw, held, sems):
    return [
        pltpu.make_async_copy(raw.at[:, i], held.at[i], sems.at[i]) for i in range(held.shape[0])
    ]


def weight_cols(held, lo, size):
    inner, outer, piece, _ = held.shape
    return held[:, :, :, pl.ds(lo, size)].reshape(inner * outer * piece, size)


def weight_rows(held, chunk):
    inner, outer, piece, cols = held.shape
    if inner % CH == 0:
        take = inner // CH
        return held[chunk * take : (chunk + 1) * take].reshape(take * outer * piece, cols)
    take = piece // CH
    return held[0, 0, chunk * take : (chunk + 1) * take, :]


def params(collective_id):
    return pltpu.CompilerParams(
        collective_id=collective_id, has_side_effects=True, vmem_limit_bytes=48 * 1024 * 1024
    )


def cost(us):
    return pl.CostEstimate(flops=0, bytes_accessed=int(us * 3.3e6), transcendentals=0)


STEP_COLS = 256


def forward_kernel(n, layer, mode, waits, *refs):
    refs = list(refs)
    lhs, w_any, res, vec = refs[:4]
    del refs[:4]
    raw = bias = None
    if mode:
        raw, bias = refs[:2]
        del refs[:2]
    del refs[:waits]
    y_ref = refs.pop(0)
    outs = []
    if mode:
        count = 3 if mode == "gelu" else 2
        outs = refs[:count]
        del refs[:count]
    w, w_sem, hold, recv, send, final, s_send, s_recv = refs[:8]
    del refs[:8]
    me = lax.axis_index("group")
    rows = res.shape[0]
    w_copy = pltpu.make_async_copy(w_any.at[layer], w, w_sem)
    w_copy.start()
    if mode:
        g_send, g_recv, held, h_sems = refs
        others = weight_copies(raw, held, h_sems)
        for other in others:
            other.start()
    greet_line(n, me)
    w_copy.wait()
    cols = w.shape[1] // CH

    def part(block, into):
        mine = lhs[rows_at(block, rows), :]
        for chunk in range(CH):
            into[chunk] = dot(mine, w[:, chunk * cols : (chunk + 1) * cols])

    line_scatter(n, me, part, hold, recv, send, final, s_send, s_recv)
    y = res[...] + joined(final) + vec[0:1, :]
    y_ref[...] = y
    if not mode:
        return
    all_ref = outs[0]
    all_ref[rows_at(me, rows), :] = norm_apply(y, vec[1:2, :], vec[2:3, :])[0].astype(B16)
    wide = held.shape[-1]
    size = STEP_COLS if wide % STEP_COLS == 0 else wide
    waited = []

    def on_block(block):
        if not waited:
            for other in others:
                other.wait()
            waited.append(True)
        here = rows_at(block, rows)

        def column(i, carry):
            lo = pl.multiple_of(i * size, size)
            value = dot(all_ref[here, :], weight_cols(held, lo, size)) + bias[:, pl.ds(lo, size)]
            if mode == "gelu":
                value, slope = gelu_parts(value)
                outs[2][here, pl.ds(lo, size)] = slope
            outs[1][here, pl.ds(lo, size)] = value.astype(B16)
            return carry

        lax.fori_loop(0, wide // size, column, 0)

    line_gather(n, me, all_ref, rows, g_send, g_recv, on_block)


def forward_step(lhs, w_all, layer, res, vec, collective_id, mode=None, raw=None, bias=None, after=()):
    n = lax.axis_size("group")
    rows, width = res.shape
    depth = w_all.shape[1]
    ins = [lhs, w_all, res, vec]
    specs = [VMEM, ANY, VMEM, VMEM]
    outs = [jax.ShapeDtypeStruct((rows, width), F32)]
    scratch = [pltpu.VMEM((depth, width), B16), pltpu.SemaphoreType.DMA] + scatter_scratch(n, rows, width)
    us = 21.0
    if mode:
        us = 42.0
        ins += [raw, bias]
        specs += [ANY, VMEM]
        wide = raw.shape[-1]
        outs += [
            jax.ShapeDtypeStruct((n * rows, width), B16),
            jax.ShapeDtypeStruct((n * rows, wide), B16),
        ]
        if mode == "gelu":
            outs.append(jax.ShapeDtypeStruct((n * rows, wide), F32))
        scratch += line_sems(n) + weight_scratch(raw)
    ins += list(after)
    specs += [ANY] * len(after)
    return pl.pallas_call(
        functools.partial(forward_kernel, n, layer, mode, len(after)),
        out_shape=outs,
        in_specs=specs,
        out_specs=[VMEM] * len(outs),
        scratch_shapes=scratch,
        compiler_params=params(collective_id),
        cost_estimate=cost(us),
        name=f"forward_{mode}_{layer}",
    )(*ins)


def backward_kernel(n, layer, mode, waits, *refs):
    refs = list(refs)
    lhs, raw, xin, gain, res = refs[:5]
    del refs[:5]
    if mode:
        w_any = refs.pop(0)
    if mode == "gelu":
        slope = refs.pop(0)
    del refs[:waits]
    g_ref, small_ref = refs[:2]
    del refs[:2]
    if mode:
        all_ref, t_ref = refs[:2]
        del refs[:2]
    if mode == "gelu":
        sum_ref = refs.pop(0)
    held, h_sems, hold, recv, send, final, s_send, s_recv = refs[:8]
    del refs[:8]
    me = lax.axis_index("group")
    rows = res.shape[0]
    others = weight_copies(raw, held, h_sems)
    for other in others:
        other.start()
    if mode:
        g_send, g_recv, w, w_sem = refs
        w_copy = pltpu.make_async_copy(w_any.at[layer], w, w_sem)
        w_copy.start()
    greet_line(n, me)
    for other in others:
        other.wait()

    def part(block, into):
        mine = lhs[rows_at(block, rows), :]
        for chunk in range(CH):
            into[chunk] = dot_nt(mine, weight_rows(held, chunk))

    line_scatter(n, me, part, hold, recv, send, final, s_send, s_recv)
    grad = joined(final)
    _, normed, inverse = norm_apply(xin[...], gain[...], gain[...])
    result = res[...] + norm_back(grad, normed, inverse, gain[...])
    g_ref[...] = result
    small_ref[0:1, :] = jnp.sum(grad * normed, axis=0, keepdims=True)
    small_ref[1:2, :] = jnp.sum(grad, axis=0, keepdims=True)
    small_ref[2:3, :] = jnp.sum(result, axis=0, keepdims=True)
    if not mode:
        return
    all_ref[rows_at(me, rows), :] = result.astype(B16)
    wide = w.shape[0]
    size = STEP_COLS if wide % STEP_COLS == 0 else wide
    if mode == "gelu":
        sum_ref[...] = jnp.zeros_like(sum_ref)
    waited = []

    def on_block(block):
        if not waited:
            w_copy.wait()
            waited.append(True)
        here = rows_at(block, rows)

        def column(i, carry):
            lo = pl.multiple_of(i * size, size)
            value = dot_nt(all_ref[here, :], w[pl.ds(lo, size), :])
            if mode == "gelu":
                value = value * slope[here, pl.ds(lo, size)]
                sum_ref[:, pl.ds(lo, size)] += jnp.sum(value, axis=0, keepdims=True)
            t_ref[here, pl.ds(lo, size)] = value.astype(B16)
            return carry

        lax.fori_loop(0, wide // size, column, 0)

    line_gather(n, me, all_ref, rows, g_send, g_recv, on_block)


def backward_step(lhs, raw, xin, gain, res, collective_id, mode=None, w_all=None, layer=0, slope=None, after=()):
    n = lax.axis_size("group")
    rows, width = res.shape
    ins = [lhs, raw, xin, gain, res]
    specs = [VMEM, ANY, VMEM, VMEM, VMEM]
    outs = [jax.ShapeDtypeStruct((rows, width), F32), jax.ShapeDtypeStruct((8, width), F32)]
    scratch = weight_scratch(raw) + scatter_scratch(n, rows, width)
    us = 21.0
    if mode:
        us = 42.0
        ins.append(w_all)
        specs.append(ANY)
        wide = w_all.shape[1]
        outs += [
            jax.ShapeDtypeStruct((n * rows, width), B16),
            jax.ShapeDtypeStruct((n * rows, wide), B16),
        ]
        scratch += line_sems(n) + [pltpu.VMEM((wide, width), B16), pltpu.SemaphoreType.DMA]
    if mode == "gelu":
        ins.append(slope)
        specs.append(VMEM)
        outs.append(jax.ShapeDtypeStruct((1, wide), F32))
    ins += list(after)
    specs += [ANY] * len(after)
    return pl.pallas_call(
        functools.partial(backward_kernel, n, layer, mode, len(after)),
        out_shape=outs,
        in_specs=specs,
        out_specs=[VMEM] * len(outs),
        scratch_shapes=scratch,
        compiler_params=params(collective_id),
        cost_estimate=cost(us),
        name=f"backward_{mode}_{layer}",
    )(*ins)


def first_kernel(n, normed, x_ref, vec, after, all_ref, g_send, g_recv):
    me = lax.axis_index("group")
    rows = x_ref.shape[0]
    greet_line(n, me)
    value = x_ref[...]
    if normed:
        value = norm_apply(value.astype(F32), vec[0:1, :], vec[1:2, :])[0].astype(B16)
    all_ref[rows_at(me, rows), :] = value
    line_gather(n, me, all_ref, rows, g_send, g_recv, lambda block: None)


def first_gather(x, vec, collective_id, normed, after):
    n = lax.axis_size("group")
    rows, width = x.shape
    return pl.pallas_call(
        functools.partial(first_kernel, n, normed),
        out_shape=jax.ShapeDtypeStruct((n * rows, width), B16),
        in_specs=[VMEM, VMEM, ANY],
        out_specs=VMEM,
        scratch_shapes=line_sems(n),
        compiler_params=params(collective_id),
        cost_estimate=cost(21.0),
        name="first_gather" if normed else "cot_gather",
    )(x, vec, after)


def swap_kernel(n, count, *refs):
    ins, outs = refs[:count], refs[count + 1 : 2 * count + 1]
    send_sems, recv_sems, own_sems = refs[2 * count + 1 :]
    me = lax.axis_index("group")
    peers = [lax.rem(me + step, n) for step in range(1, n)]
    barrier = pltpu.get_barrier_semaphore()
    for peer in peers:
        pl.semaphore_signal(barrier, inc=1, device_id={"group": peer}, device_id_type=MESH)
    pl.semaphore_wait(barrier, n - 1)
    copies = []
    for k in range(count):
        for step, peer in enumerate(peers):
            copy = pltpu.make_async_remote_copy(
                src_ref=ins[k].at[peer],
                dst_ref=outs[k].at[me],
                send_sem=send_sems.at[k, step],
                recv_sem=recv_sems.at[k, step],
                device_id={"group": peer},
                device_id_type=MESH,
            )
            copy.start()
            copies.append(copy)
        own = pltpu.make_async_copy(ins[k].at[me], outs[k].at[me], own_sems.at[k])
        own.start()
        copies.append(own)
    for copy in copies:
        copy.wait()


def swap(blocks, collective_id, after=None, us=8.0):
    n = lax.axis_size("group")
    count = len(blocks)
    return pl.pallas_call(
        functools.partial(swap_kernel, n, count),
        out_shape=[jax.ShapeDtypeStruct(b.shape, b.dtype) for b in blocks],
        in_specs=[VMEM] * count + [ANY],
        out_specs=[VMEM] * count,
        scratch_shapes=[pltpu.SemaphoreType.DMA((count, n - 1)) for _ in range(2)]
        + [pltpu.SemaphoreType.DMA((count,))],
        compiler_params=params(collective_id),
        cost_estimate=cost(us),
        name=f"swap_{collective_id}",
    )(*blocks, blocks[0] if after is None else after)


def grads_kernel(n, a_ref, b_ref, c_ref, d_ref, o_ref, held, sems):
    own = held.shape[0]
    cols, width = b_ref.shape[1], d_ref.shape[1]
    folds = c_ref.shape[1] // own
    copies = []
    for i in range(n + folds):
        if i < n:
            lo, size = i * cols, cols
            value = dot_tn(a_ref[:, i * own : (i + 1) * own], b_ref[...])
        else:
            lo, size = n * cols + (i - n) * width, width
            value = dot_tn(c_ref[:, (i - n) * own : (i - n + 1) * own], d_ref[...])
        held[:, lo : lo + size] = value.astype(B16)
        copy = pltpu.make_async_copy(
            held.at[:, pl.ds(lo, size)], o_ref.at[:, pl.ds(lo, size)], sems.at[i]
        )
        copy.start()
        copies.append(copy)
    for copy in copies:
        copy.wait()


def grads_pair(a, b, c, d):
    n = lax.axis_size("group")
    own = a.shape[1] // n
    folds = c.shape[1] // own
    total = n * b.shape[1] + folds * d.shape[1]
    return pl.pallas_call(
        functools.partial(grads_kernel, n),
        out_shape=jax.ShapeDtypeStruct((own, total), B16),
        in_specs=[VMEM] * 4,
        out_specs=ANY,
        scratch_shapes=[pltpu.VMEM((own, total), B16), pltpu.SemaphoreType.DMA((n + folds,))],
        compiler_params=pltpu.CompilerParams(vmem_limit_bytes=32 * 1024 * 1024),
        cost_estimate=cost(4.0),
        name="weight_grads",
    )(a, b, c, d)


def digit(value, place):
    return (value // 2**place) % 2


def with_digit(value, place, wanted):
    return value + (wanted - digit(value, place)) * 2**place


def flipped(value, place):
    return value + (1 - 2 * digit(value, place)) * 2**place


def reduce_share_kernel(n, replicas, cols, minor, g_ref, after, o_ref, *refs):
    own_half, first_in, acc, flow_in, landed = refs[:5]
    sems = refs[5:]
    pair_send, pair_recv, flow_send, flow_recv, swap_send, swap_recv = sems[:6]
    out_send, out_recv, side_send, side_recv, load_sems = sems[6:]
    me = lax.axis_index("group")
    mine = lax.axis_index("replica")
    core = digit(mine, 0)
    spot = mine // 2
    halves = replicas // 2
    bits = halves.bit_length() - 1
    total = g_ref.shape[2]
    flow_cols = total // 2
    orders = (list(range(bits)), list(range(bits))[::-1])
    sibling = flipped(mine, 0)
    peers = [lax.rem(me + step, n) for step in range(1, n)]
    barrier = pltpu.get_barrier_semaphore()
    for place in range(bits + 1):
        pl.semaphore_signal(
            barrier, inc=1, device_id={"replica": flipped(mine, place)}, device_id_type=MESH
        )
    for peer in peers:
        pl.semaphore_signal(barrier, inc=1, device_id={"group": peer}, device_id_type=MESH)
    loads = []
    for q in range(halves):
        load = pltpu.make_async_copy(g_ref.at[2 * q + core], own_half.at[q], load_sems.at[q])
        load.start()
        loads.append(load)
    pl.semaphore_wait(barrier, bits + n)

    def to_replica(src, dst, send_sem, recv_sem, target):
        copy = pltpu.make_async_remote_copy(
            src_ref=src,
            dst_ref=dst,
            send_sem=send_sem,
            recv_sem=recv_sem,
            device_id={"replica": target},
            device_id_type=MESH,
        )
        copy.start()
        return copy

    sent = []
    paired = []
    for q in range(halves):
        copy = to_replica(
            g_ref.at[2 * q + 1 - core], first_in.at[q], pair_send.at[q], pair_recv.at[q], sibling
        )
        paired.append(copy)
    sent += paired
    for q in range(halves):
        loads[q].wait()
        paired[q].wait_recv()
        acc[q] = (own_half[q].astype(F32) + first_in[q].astype(F32)).astype(B16)

    def chosen(order, count, index):
        spot_of = spot
        for i in range(count):
            spot_of = with_digit(spot_of, order[i], (index >> i) % 2)
        return spot_of

    slot = 0
    for stage in range(bits):
        started = []
        for flow in (0, 1):
            lanes = pl.ds(flow * flow_cols, flow_cols)
            place = orders[flow][stage]
            free = orders[flow][stage + 1 :]
            for t in range(2 ** len(free)):
                keep = chosen(free, len(free), t)
                copy = to_replica(
                    acc.at[flipped(keep, place), :, lanes],
                    flow_in.at[flow, slot + t],
                    flow_send.at[flow, slot + t],
                    flow_recv.at[flow, slot + t],
                    flipped(mine, place + 1),
                )
                started.append((copy, flow, slot + t, keep))
        for copy, flow, at, keep in started:
            copy.wait_recv()
            lanes = slice(flow * flow_cols, (flow + 1) * flow_cols)
            acc[keep, :, lanes] = (
                acc[keep, :, lanes].astype(F32) + flow_in[flow, at].astype(F32)
            ).astype(B16)
            sent.append(copy)
        slot += 2 ** (bits - 1 - stage)

    swaps = []
    for step, peer in enumerate(peers):
        copy = pltpu.make_async_remote_copy(
            src_ref=acc.at[spot, :, pl.ds(pl.multiple_of(peer * cols, 128), cols)],
            dst_ref=landed.at[me],
            send_sem=swap_send.at[step],
            recv_sem=swap_recv.at[step],
            device_id={"group": peer},
            device_id_type=MESH,
        )
        copy.start()
        swaps.append(copy)
    landed[me] = acc[spot, :, pl.ds(pl.multiple_of(me * cols, 128), cols)]
    o_ref[mine, :, n * cols :] = acc[spot, :, n * cols :]
    for copy in swaps:
        copy.wait_recv()
    sent += swaps
    inner = cols // minor
    for src in range(n):
        for m in range(minor):
            lo = (m * n + src) * inner
            o_ref[mine, :, lo : lo + inner] = landed[src, :, m * inner : (m + 1) * inner]

    def place_out(spot_of, flow):
        return o_ref.at[2 * spot_of + core, :, pl.ds(flow * flow_cols, flow_cols)]

    sides = []

    def to_side(spot_of, flow, index):
        here = place_out(spot_of, flow)
        sides.append(
            to_replica(here, here, side_send.at[flow, index], side_recv.at[flow, index], sibling)
        )

    slot = 0
    for stage in range(bits):
        started = []
        for flow in (0, 1):
            order = orders[flow][::-1]
            place = order[stage]
            for t in range(2**stage):
                here = place_out(chosen(order, stage, t), flow)
                copy = to_replica(
                    here,
                    here,
                    out_send.at[flow, slot + t],
                    out_recv.at[flow, slot + t],
                    flipped(mine, place + 1),
                )
                started.append((copy, flow, t))
        if stage == 0:
            for flow in (0, 1):
                to_side(spot, flow, 0)
        for copy, flow, t in started:
            order = orders[flow][::-1]
            copy.wait_recv()
            to_side(flipped(chosen(order, stage, t), order[stage]), flow, 2**stage + t)
            sent.append(copy)
        slot += 2**stage
    for copy in sides:
        copy.wait_recv()
    for copy in sent + sides:
        copy.wait_send()


def reduce_share(grads, cols, minor, collective_id, after):
    n, replicas = lax.axis_size("group"), lax.axis_size("replica")
    own, total = grads.shape
    piece, halves = own // replicas, replicas // 2
    dma = lambda *shape: pltpu.SemaphoreType.DMA(shape)
    full = pl.pallas_call(
        functools.partial(reduce_share_kernel, n, replicas, cols, minor),
        out_shape=jax.ShapeDtypeStruct((replicas, piece, total), B16),
        in_specs=[ANY, ANY],
        out_specs=VMEM,
        scratch_shapes=[
            pltpu.VMEM((halves, piece, total), B16),
            pltpu.VMEM((halves, piece, total), B16),
            pltpu.VMEM((halves, piece, total), B16),
            pltpu.VMEM((2, halves - 1, piece, total // 2), B16),
            pltpu.VMEM((n, piece, cols), B16),
            dma(halves),
            dma(halves),
            dma(2, halves),
            dma(2, halves),
            dma(n - 1),
            dma(n - 1),
            dma(2, halves),
            dma(2, halves),
            dma(2, halves),
            dma(2, halves),
            dma(halves),
        ],
        compiler_params=params(collective_id),
        cost_estimate=cost(35.0),
        name="reduce_share",
    )(grads.reshape(replicas, piece, total), after)
    return full.reshape(own, total)


def small_sums_kernel(n, replicas, wide, ups, o_ref, landed, both, spread, *sems):
    a_send, a_recv, b_send, b_recv = sems
    me = lax.axis_index("group")
    mine = lax.axis_index("replica")
    rows = landed.shape[1]
    peers = [lax.rem(me + step, n) for step in range(1, n)]
    mates = [lax.rem(mine + step, replicas) for step in range(1, replicas)]
    barrier = pltpu.get_barrier_semaphore()
    for peer in peers:
        pl.semaphore_signal(barrier, inc=1, device_id={"group": peer}, device_id_type=MESH)
    for mate in mates:
        pl.semaphore_signal(barrier, inc=1, device_id={"replica": mate}, device_id_type=MESH)
    pl.semaphore_wait(barrier, n + replicas - 2)
    copies = []
    for step, peer in enumerate(peers):
        copy = pltpu.make_async_remote_copy(
            src_ref=wide.at[peer],
            dst_ref=landed.at[me],
            send_sem=a_send.at[step],
            recv_sem=a_recv.at[step],
            device_id={"group": peer},
            device_id_type=MESH,
        )
        copy.start()
        copies.append(copy)
    landed[me] = wide[me]
    for copy in copies:
        copy.wait_recv()
    total = landed[0]
    for i in range(1, n):
        total = total + landed[i]
    both[0:rows, :] = total
    both[rows:, :] = ups[...]
    spread[mine] = both[...]
    others = []
    for step, mate in enumerate(mates):
        copy = pltpu.make_async_remote_copy(
            src_ref=both,
            dst_ref=spread.at[mine],
            send_sem=b_send.at[step],
            recv_sem=b_recv.at[step],
            device_id={"replica": mate},
            device_id_type=MESH,
        )
        copy.start()
        others.append(copy)
    for copy in others:
        copy.wait_recv()
    total = spread[0]
    for i in range(1, replicas):
        total = total + spread[i]
    o_ref[...] = total
    for copy in copies + others:
        copy.wait_send()


def small_sums(wide, ups, collective_id):
    n, replicas = lax.axis_size("group"), lax.axis_size("replica")
    _, rows, own = wide.shape
    lines = rows + ups.shape[0]
    return pl.pallas_call(
        functools.partial(small_sums_kernel, n, replicas),
        out_shape=jax.ShapeDtypeStruct((lines, own), F32),
        in_specs=[VMEM, VMEM],
        out_specs=VMEM,
        scratch_shapes=[
            pltpu.VMEM((n, rows, own), F32),
            pltpu.VMEM((lines, own), F32),
            pltpu.VMEM((replicas, lines, own), F32),
            pltpu.SemaphoreType.DMA((n - 1,)),
            pltpu.SemaphoreType.DMA((n - 1,)),
            pltpu.SemaphoreType.DMA((replicas - 1,)),
            pltpu.SemaphoreType.DMA((replicas - 1,)),
        ],
        compiler_params=params(collective_id),
        cost_estimate=cost(9.0),
        name="small_sums",
    )(wide, ups)


def attention(q, k, v, first_head, heads_here):
    tokens = q.shape[0]
    split = lambda m: m.reshape(tokens, heads_here, HEAD_DIM).transpose(1, 0, 2)
    q, k, v = split(q), split(k), split(v)
    head_ids = (first_head + jnp.arange(heads_here, dtype=jnp.int32)).astype(F32)
    slopes = 2.0 ** (-8.0 * (head_ids + 1.0) / HEADS)
    pos = jnp.arange(tokens, dtype=jnp.int32)
    offset = (pos[:, None] - pos[None, :]).astype(F32)
    raw = jnp.einsum("hqd,hkd->hqk", q, k, preferred_element_type=F32)
    scores = raw * HEAD_DIM ** (-0.5) - slopes[:, None, None] * offset[None]
    scores = jnp.where((offset >= 0.0)[None], scores, NEG)
    row_top = jnp.max(scores, axis=-1, keepdims=True)
    exps_raw = jnp.exp(scores - row_top)
    row_total = jnp.sum(exps_raw, axis=-1, keepdims=True)
    probs = (exps_raw * (1.0 / row_total)).astype(B16)
    context = jnp.einsum("hqk,hkd->hqd", probs, v, preferred_element_type=F32).astype(B16)
    return context.transpose(1, 0, 2).reshape(tokens, -1), (q, k, v, probs, context)


def attention_back(d_context, saved):
    q, k, v, probs, context = saved
    heads_here, tokens, _ = q.shape
    dc = d_context.reshape(tokens, heads_here, HEAD_DIM).transpose(1, 0, 2)
    d_probs = jnp.einsum("hqd,hkd->hqk", dc, v, preferred_element_type=F32)
    delta = jnp.sum(dc.astype(F32) * context.astype(F32), axis=-1, keepdims=True)
    ds = (probs.astype(F32) * (d_probs - delta)).astype(B16)
    scale = HEAD_DIM ** (-0.5)
    dq = jnp.einsum("hqk,hkd->hqd", ds, k, preferred_element_type=F32) * scale
    dk = jnp.einsum("hqk,hqd->hkd", ds, q, preferred_element_type=F32) * scale
    dv = jnp.einsum("hqk,hqd->hkd", probs, dc, preferred_element_type=F32)
    sums = (jnp.sum(dq, axis=1).reshape(-1), jnp.sum(dv, axis=1).reshape(-1))
    join = lambda m: m.astype(B16).transpose(1, 0, 2).reshape(tokens, -1)
    return jnp.concatenate([join(dq), join(dk), join(dv)], axis=1), sums


def local(
    inputs,
    cotangent,
    norm_gain,
    norm_bias,
    w_qkv,
    bias_qv,
    w_out,
    bias_out,
    w_up,
    bias_up,
    w_down,
    bias_down,
):
    groups = lax.axis_size("group")
    replicas = lax.axis_size("replica")
    me = lax.axis_index("group")
    copy_idx = lax.axis_index("replica")
    layers, own, _ = w_qkv.shape
    width = own * groups
    ff_own = w_down.shape[1]
    heads_here = HEADS // groups
    piece = own // replicas

    qkv_piece = lax.dynamic_slice_in_dim(w_qkv, copy_idx * piece, piece, axis=1)
    qkv_piece = qkv_piece.reshape(layers, piece, 3, groups, own).transpose(0, 3, 1, 2, 4)
    qkv_piece = qkv_piece.reshape(layers, groups, piece, 3 * own)
    up_piece = lax.dynamic_slice_in_dim(w_up, copy_idx * piece, piece, axis=1)
    up_piece = up_piece.reshape(layers, piece, groups, ff_own).transpose(0, 2, 1, 3)

    def share(block):
        full = lax.all_gather(block, "replica", axis=0)
        if piece % 16:
            full = full.transpose(1, 0, 2, 3).reshape(1, 1, width, -1)
        return full

    small = jnp.concatenate(
        [norm_gain, norm_bias, bias_qv.reshape(layers, 2, own), bias_out[:, None], bias_down[:, None]],
        axis=1,
    ).reshape(layers * 8, own)
    small = jnp.broadcast_to(small[None], (groups,) + small.shape)
    small, wq_first = swap([small, qkv_piece[0]], 0)
    wq = [share(wq_first)] + [None] * (layers - 1)
    wu = [None] * layers

    small = small.reshape(groups, layers, 8, own).astype(F32)
    rows_of = lambda i: small[:, :, i].transpose(1, 0, 2).reshape(layers, width)
    gains = [rows_of(0), rows_of(1)]
    shifts = [rows_of(2), rows_of(3)]
    qv_full = small[:, :, 4:6].transpose(1, 0, 2, 3).reshape(layers, 2 * width)
    q_bias = lax.dynamic_slice_in_dim(qv_full, me * own, own, axis=1)
    v_bias = lax.dynamic_slice_in_dim(qv_full, width + me * own, own, axis=1)
    qkv_bias = jnp.concatenate([q_bias, jnp.zeros_like(q_bias), v_bias], axis=1)
    out_bias, down_bias = rows_of(6), rows_of(7)
    up_bias = bias_up.astype(F32)

    x = inputs[0].astype(F32)
    vec0 = jnp.stack([gains[0][0], shifts[0][0]])
    a1_all = first_gather(inputs[0], vec0, 1, True, wq_first)
    later = [up_piece[l] for l in range(layers)] + [qkv_piece[l] for l in range(1, layers)]
    later = swap(later, 2, a1_all, 24.0)
    for l in range(layers):
        wu[l] = share(later[l])
        if l:
            wq[l] = share(later[layers + l - 1])
    cot_all = first_gather(cotangent[0], vec0, 3, False, later[0])

    full0 = wq[0].transpose(1, 0, 2, 3).reshape(width, 3 * own)
    proj = (dot(a1_all, full0) + qkv_bias[0]).astype(B16)
    kept = []
    for l in range(layers):
        cut = lambda i: proj[:, i * own : (i + 1) * own]
        context, attn_saved = attention(cut(0), cut(1), cut(2), me * heads_here, heads_here)
        vec = jnp.stack([out_bias[l], gains[1][l], shifts[1][l]])
        h, a2_all, hidden, slope = forward_step(
            context, w_out, l, x, vec, 10 + 4 * l, "gelu", wu[l], up_bias[l][None]
        )
        saved = (x, a1_all, attn_saved, context, h, a2_all, slope, hidden)
        if l + 1 < layers:
            vec = jnp.stack([down_bias[l], gains[0][l + 1], shifts[0][l + 1]])
            x, a1_all, proj = forward_step(
                hidden, w_down, l, h, vec, 11 + 4 * l, "bias", wq[l + 1], qkv_bias[l + 1][None]
            )
        else:
            vec = jnp.stack([down_bias[l], down_bias[l], down_bias[l]])
            (x,) = forward_step(hidden, w_down, l, h, vec, 11 + 4 * l)
        kept.append(saved)
    outputs = x.astype(B16)[None]

    def reduce_pair(grads):
        return lax.psum_scatter(grads, "replica", scatter_dimension=0, tiled=True)

    def swap_pair(mine, cols, collective_id, after=None):
        cut = groups * cols
        left = mine[:, :cut].reshape(piece, groups, cols).transpose(1, 0, 2)
        return swap([left], collective_id, after)[0]

    def share_pair(left, mine, cols, minor):
        cut = groups * cols
        left = left.reshape(groups, piece, minor, cols // minor).transpose(1, 2, 0, 3)
        mine = jnp.concatenate([left.reshape(piece, cut), mine[:, cut:]], axis=1)
        return lax.all_gather(mine, "replica", axis=0, tiled=True)

    def unpack_pair(full, cols):
        cut = groups * cols
        folds = (full.shape[1] - cut) // width
        rows = [full[:, cut + i * width : cut + (i + 1) * width] for i in range(folds)]
        return full[:, :cut].astype(F32), jnp.concatenate(rows, axis=0).astype(F32)

    g = cotangent[0].astype(F32)
    g_sum = jnp.sum(g, axis=0)
    g_all = cot_all
    smalls = [None] * layers
    ffn_sum = [None] * layers
    attn_sum = [None] * layers
    ffn_full = [None] * layers
    attn_full = [None] * layers
    zeros_qv = jnp.zeros((2 * width,), F32)
    pre = up_sum = None
    waits = ()
    for l in reversed(range(layers)):
        x_in, a1_all, attn_saved, context, h, a2_all, slope, hidden = kept[l]
        if pre is None:
            d_pre = dot_nt(g_all, w_down[l]) * slope
            up_sum = jnp.sum(d_pre, axis=0)
            pre = d_pre.astype(B16)
        ffn_grads = grads_pair(a2_all, pre, hidden, g_all)
        ffn_sum[l] = reduce_pair(ffn_grads)
        down_sum, ups = g_sum, up_sum
        dh, small1, dh_all, dc = backward_step(
            pre, wu[l], h, gains[1][l][None], g, 30 + 4 * l, "plain", w_out, l, after=(ffn_grads,) + waits
        )
        d_proj, (dq_sum, dv_sum) = attention_back(dc, attn_saved)
        attn_grads = grads_pair(a1_all, d_proj, context, dh_all)
        if l:
            attn_sum[l] = reduce_pair(attn_grads)
            ffn_left = swap_pair(ffn_sum[l], ff_own, 60 + 4 * l, attn_grads)
            ffn_full[l] = share_pair(ffn_left, ffn_sum[l], ff_own, 1)
            g, small0, g_all, pre, up_sum = backward_step(
                d_proj, wq[l], x_in, gains[0][l][None], dh, 31 + 4 * l, "gelu", w_down, l - 1, kept[l - 1][6],
                after=(attn_grads, ffn_left),
            )
            attn_left = swap_pair(attn_sum[l], 3 * own, 61 + 4 * l, small0)
            attn_full[l] = share_pair(attn_left, attn_sum[l], 3 * own, 3)
            waits = (attn_left,)
            g_sum, up_sum = small0[2], up_sum[0]
        else:
            g, small0 = backward_step(
                d_proj, wq[l], x_in, gains[0][l][None], dh, 31 + 4 * l, after=(attn_grads,)
            )
            ffn_left = swap_pair(ffn_sum[l], ff_own, 60 + 4 * l, small0)
            ffn_full[l] = share_pair(ffn_left, ffn_sum[l], ff_own, 1)
            attn_full[l] = reduce_share(attn_grads, 3 * own, 3, 70, ffn_left)
        qv = lax.dynamic_update_slice_in_dim(zeros_qv, dq_sum, me * own, axis=0)
        qv = lax.dynamic_update_slice_in_dim(qv, dv_sum, width + me * own, axis=0)
        smalls[l] = (
            jnp.concatenate([small0[0], small1[0], small0[1], small1[1], qv, small1[2], down_sum]),
            ups,
        )

    grads = [unpack_pair(attn_full[l], 3 * own) + unpack_pair(ffn_full[l], ff_own) for l in range(layers)]

    wide = jnp.stack([s[0] for s in smalls])
    per_owner = lambda lo, n: wide[:, lo * width : (lo + n) * width].reshape(layers, n, groups, own)
    gain_bias = per_owner(0, 4).transpose(2, 0, 1, 3)
    qv = wide[:, 4 * width : 6 * width].reshape(layers, groups, 2, own).transpose(1, 0, 2, 3)
    dense = per_owner(6, 2).transpose(2, 0, 1, 3)
    wide = jnp.concatenate([gain_bias, qv, dense], axis=2)
    ups = jnp.stack([s[1] for s in smalls]).reshape(-1, own)
    total = small_sums(wide.reshape(groups, layers * 8, own), ups, 5)
    own_cols = total[: layers * 8].reshape(layers, 8, own)
    up_total = total[layers * 8 :].reshape(layers, ff_own)
    qv_total = own_cols[:, 4:6].reshape(layers, 2 * own)
    stack = lambda i: jnp.stack([grads[l][i] for l in range(layers)])
    return (
        outputs,
        g[None],
        own_cols[:, 0:2],
        own_cols[:, 2:4],
        stack(0),
        qv_total,
        stack(1),
        own_cols[:, 6],
        stack(2),
        up_total,
        stack(3),
        own_cols[:, 7],
    )


def solution(mesh):
    rows = P("replica", "group", None)
    vec = P(None, None, "group")
    mat = P(None, "group", None)
    bias = P(None, "group")
    params_in = (vec, vec, mat, bias, mat, bias, mat, bias, mat, bias)
    return jax.shard_map(
        local,
        mesh=mesh,
        in_specs=(rows, rows) + params_in,
        out_specs=(rows, rows) + params_in,
        check_vma=False,
    )
```

```python
import functools

import jax
import jax.numpy as jnp
from jax import lax
from jax.experimental import pallas as pl
from jax.experimental.pallas import tpu as pltpu
from jax.sharding import PartitionSpec as P

HEADS = 16
HEAD_DIM = 64

EPS = 1e-05
NEG = -1e30
GELU_C = 0.7978845608028654
GELU_A = 0.044715
F32 = jnp.float32
B16 = jnp.bfloat16
MESH = pl.DeviceIdType.MESH
CH = 2

VMEM = pl.BlockSpec(memory_space=pltpu.VMEM)
ANY = pl.BlockSpec(memory_space=pl.ANY)


def norm_apply(values_in, gain_row, bias_row):
    row_mean = jnp.mean(values_in, axis=-1, keepdims=True)
    centered = values_in - row_mean
    variance = jnp.mean(centered * centered, axis=-1, keepdims=True)
    inverse = lax.rsqrt(variance + EPS)
    normed = centered * inverse
    return (normed * gain_row + bias_row, normed, inverse)


def norm_back(grad_in, normed, inverse, gain_row):
    scaled = grad_in * gain_row
    return inverse * (
        scaled
        - jnp.mean(scaled, axis=-1, keepdims=True)
        - normed * jnp.mean(scaled * normed, axis=-1, keepdims=True)
    )


def gelu_parts(pre_act):
    tanh_val = jnp.tanh(GELU_C * (pre_act + GELU_A * pre_act * pre_act * pre_act))
    gelu_value = 0.5 * pre_act * (1.0 + tanh_val)
    gelu_slope = 0.5 * (1.0 + tanh_val) + 0.5 * pre_act * (1.0 - tanh_val * tanh_val) * GELU_C * (
        1.0 + 3.0 * GELU_A * pre_act * pre_act
    )
    return (gelu_value, gelu_slope)


def dot(a, b):
    return jnp.dot(a, b, preferred_element_type=F32)


def dot_nt(a, b):
    return lax.dot_general(a, b, (((1,), (1,)), ((), ())), preferred_element_type=F32)


def dot_tn(a, b):
    return lax.dot_general(a, b, (((0,), (0,)), ((), ())), preferred_element_type=F32)


def greet_line(n, me):
    barrier = pltpu.get_barrier_semaphore()
    for there, peer in ((me > 0, me - 1), (me < n - 1, me + 1)):

        @pl.when(there)
        def _():
            pl.semaphore_signal(barrier, inc=1, device_id={"group": peer}, device_id_type=MESH)

    beside_me = (me > 0).astype(jnp.int32) + (me < n - 1).astype(jnp.int32)
    pl.semaphore_wait(barrier, beside_me)


def beside(way, me):
    return me + 1 if way == 0 else me - 1


def line_gather(n, me, buf, rows, send_sems, recv_sems, on_block):
    part = rows // CH

    def copy(way, step, chunk, block):
        here = pl.ds(pl.multiple_of(block * rows + chunk * part, part), part)
        return pltpu.make_async_remote_copy(
            src_ref=buf.at[here],
            dst_ref=buf.at[here],
            send_sem=send_sems.at[way, step, chunk],
            recv_sem=recv_sems.at[way, step, chunk],
            device_id={"group": beside(way, me)},
            device_id_type=MESH,
        )

    def block_of(way, step):
        return me - step if way == 0 else me + step

    def have(way, step):
        return me - step >= 0 if way == 0 else me + step < n

    def onward(way):
        return me < n - 1 if way == 0 else me > 0

    for chunk in range(CH):
        for way in (0, 1):

            @pl.when(onward(way))
            def _():
                copy(way, 0, chunk, me).start()

    on_block(me)

    def advance(step, carry):
        for chunk in range(CH):
            for way in (0, 1):

                @pl.when(have(way, step))
                def _():
                    copy(way, step - 1, chunk, block_of(way, step)).wait_recv()

                @pl.when(have(way, step) & onward(way) & (step < n - 1))
                def _():
                    copy(way, step, chunk, block_of(way, step)).start()

        for way in (0, 1):

            @pl.when(have(way, step))
            def _():
                on_block(block_of(way, step))

        return carry

    lax.fori_loop(1, n, advance, 0)

    def drain(step, carry):
        for way in (0, 1):

            @pl.when(have(way, step) & onward(way))
            def _():
                for chunk in range(CH):
                    copy(way, step, chunk, block_of(way, step)).wait_send()

        return carry

    lax.fori_loop(0, n - 1, drain, 0)


def line_scatter(n, me, part, hold, recv, send, final, send_sems, recv_sems, hook=None):
    def copy(way, step, chunk):
        return pltpu.make_async_remote_copy(
            src_ref=send.at[way, step, chunk],
            dst_ref=recv.at[way, step, chunk],
            send_sem=send_sems.at[way, step, chunk],
            recv_sem=recv_sems.at[way, step, chunk],
            device_id={"group": beside(way, me)},
            device_id_type=MESH,
        )

    def goal(way, step):
        return n - 1 - step if way == 0 else step

    def onward(way, step):
        return goal(way, step) > me if way == 0 else goal(way, step) < me

    def fed(way):
        return me > 0 if way == 0 else me < n - 1

    def advance(step, carry):
        for way in (0, 1):
            on = onward(way, step)

            @pl.when(on)
            def _():
                part(goal(way, step), hold)
                for chunk in range(CH):

                    @pl.when(fed(way))
                    def _():
                        copy(way, step, chunk).wait_recv()
                        send[way, step, chunk] = (hold[chunk] + recv[way, step, chunk].astype(F32)).astype(B16)

                    @pl.when(jnp.logical_not(fed(way)))
                    def _():
                        send[way, step, chunk] = hold[chunk].astype(B16)

                    copy(way, step, chunk).start()

        return carry

    if hook is None:
        lax.fori_loop(0, n - 1, advance, 0)
    else:
        for step in range(n - 1):
            advance(step, 0)
            hook(step)
    part(me, final)

    def collect(step, carry):
        for way in (0, 1):

            @pl.when((goal(way, step) == me) & fed(way))
            def _():
                for chunk in range(CH):
                    copy(way, step, chunk).wait_recv()
                    final[chunk] = final[chunk] + recv[way, step, chunk].astype(F32)

            @pl.when(onward(way, step))
            def _():
                for chunk in range(CH):
                    copy(way, step, chunk).wait_send()

        return carry

    lax.fori_loop(0, n - 1, collect, 0)


def line_sems(n):
    return [pltpu.SemaphoreType.DMA((2, n - 1, CH)) for _ in range(2)]


def scatter_scratch(n, rows, width):
    cols = width // CH
    return [
        pltpu.VMEM((CH, rows, cols), F32),
        pltpu.VMEM((2, n - 1, CH, rows, cols), B16),
        pltpu.VMEM((2, n - 1, CH, rows, cols), B16),
        pltpu.VMEM((CH, rows, cols), F32),
    ] + line_sems(n)


def rows_at(block, rows):
    return pl.ds(pl.multiple_of(block * rows, rows), rows)


def joined(final):
    return jnp.concatenate([final[chunk] for chunk in range(CH)], axis=1)


def weight_scratch(raw):
    outer, inner, piece, cols = raw.shape
    return [pltpu.VMEM((inner, outer, piece, cols), raw.dtype), pltpu.SemaphoreType.DMA((inner,))]


def weight_copies(raw, held, sems):
    return [
        pltpu.make_async_copy(raw.at[:, i], held.at[i], sems.at[i]) for i in range(held.shape[0])
    ]


def weight_cols(held, lo, size):
    inner, outer, piece, _ = held.shape
    return held[:, :, :, pl.ds(lo, size)].reshape(inner * outer * piece, size)


def weight_rows(held, chunk):
    inner, outer, piece, cols = held.shape
    if inner % CH == 0:
        take = inner // CH
        return held[chunk * take : (chunk + 1) * take].reshape(take * outer * piece, cols)
    take = piece // CH
    return held[0, 0, chunk * take : (chunk + 1) * take, :]


def params(collective_id):
    return pltpu.CompilerParams(
        collective_id=collective_id, has_side_effects=True, vmem_limit_bytes=48 * 1024 * 1024
    )


def cost(us):
    return pl.CostEstimate(flops=0, bytes_accessed=int(us * 3.3e6), transcendentals=0)


STEP_COLS = 256


def forward_kernel(n, layer, mode, waits, *refs):
    refs = list(refs)
    lhs, w_any, res, vec = refs[:4]
    del refs[:4]
    raw = bias = None
    if mode:
        raw, bias = refs[:2]
        del refs[:2]
    del refs[:waits]
    y_ref = refs.pop(0)
    outs = []
    if mode:
        count = 3 if mode == "gelu" else 2
        outs = refs[:count]
        del refs[:count]
    w, w_sem, hold, recv, send, final, s_send, s_recv = refs[:8]
    del refs[:8]
    me = lax.axis_index("group")
    rows = res.shape[0]
    w_copy = pltpu.make_async_copy(w_any.at[layer], w, w_sem)
    w_copy.start()
    if mode:
        g_send, g_recv, held, h_sems = refs
        others = weight_copies(raw, held, h_sems)
        for other in others:
            other.start()
    greet_line(n, me)
    w_copy.wait()
    cols = w.shape[1] // CH

    def part(block, into):
        mine = lhs[rows_at(block, rows), :]
        for chunk in range(CH):
            into[chunk] = dot(mine, w[:, chunk * cols : (chunk + 1) * cols])

    line_scatter(n, me, part, hold, recv, send, final, s_send, s_recv)
    y = res[...] + joined(final) + vec[0:1, :]
    y_ref[...] = y
    if not mode:
        return
    all_ref = outs[0]
    all_ref[rows_at(me, rows), :] = norm_apply(y, vec[1:2, :], vec[2:3, :])[0].astype(B16)
    wide = held.shape[-1]
    size = STEP_COLS if wide % STEP_COLS == 0 else wide
    waited = []

    def on_block(block):
        if not waited:
            for other in others:
                other.wait()
            waited.append(True)
        here = rows_at(block, rows)

        def column(i, carry):
            lo = pl.multiple_of(i * size, size)
            value = dot(all_ref[here, :], weight_cols(held, lo, size)) + bias[:, pl.ds(lo, size)]
            if mode == "gelu":
                value, slope = gelu_parts(value)
                outs[2][here, pl.ds(lo, size)] = slope
            outs[1][here, pl.ds(lo, size)] = value.astype(B16)
            return carry

        lax.fori_loop(0, wide // size, column, 0)

    line_gather(n, me, all_ref, rows, g_send, g_recv, on_block)


def forward_step(lhs, w_all, layer, res, vec, collective_id, mode=None, raw=None, bias=None, after=()):
    n = lax.axis_size("group")
    rows, width = res.shape
    depth = w_all.shape[1]
    ins = [lhs, w_all, res, vec]
    specs = [VMEM, ANY, VMEM, VMEM]
    outs = [jax.ShapeDtypeStruct((rows, width), F32)]
    scratch = [pltpu.VMEM((depth, width), B16), pltpu.SemaphoreType.DMA] + scatter_scratch(n, rows, width)
    us = 21.0
    if mode:
        us = 42.0
        ins += [raw, bias]
        specs += [ANY, VMEM]
        wide = raw.shape[-1]
        outs += [
            jax.ShapeDtypeStruct((n * rows, width), B16),
            jax.ShapeDtypeStruct((n * rows, wide), B16),
        ]
        if mode == "gelu":
            outs.append(jax.ShapeDtypeStruct((n * rows, wide), F32))
        scratch += line_sems(n) + weight_scratch(raw)
    ins += list(after)
    specs += [ANY] * len(after)
    return pl.pallas_call(
        functools.partial(forward_kernel, n, layer, mode, len(after)),
        out_shape=outs,
        in_specs=specs,
        out_specs=[VMEM] * len(outs),
        scratch_shapes=scratch,
        compiler_params=params(collective_id),
        cost_estimate=cost(us),
        name=f"forward_{mode}_{layer}",
    )(*ins)


def backward_kernel(n, layer, mode, waits, *refs):
    refs = list(refs)
    lhs, raw, xin, gain, res = refs[:5]
    del refs[:5]
    if mode:
        w_any = refs.pop(0)
    if mode == "gelu":
        slope = refs.pop(0)
    del refs[:waits]
    g_ref, small_ref = refs[:2]
    del refs[:2]
    if mode:
        all_ref, t_ref = refs[:2]
        del refs[:2]
    if mode == "gelu":
        sum_ref = refs.pop(0)
    held, h_sems, hold, recv, send, final, s_send, s_recv = refs[:8]
    del refs[:8]
    me = lax.axis_index("group")
    rows = res.shape[0]
    others = weight_copies(raw, held, h_sems)
    for other in others:
        other.start()
    if mode:
        g_send, g_recv, w, w_sem = refs
        w_copy = pltpu.make_async_copy(w_any.at[layer], w, w_sem)
        w_copy.start()
    greet_line(n, me)
    for other in others:
        other.wait()

    def part(block, into):
        mine = lhs[rows_at(block, rows), :]
        for chunk in range(CH):
            into[chunk] = dot_nt(mine, weight_rows(held, chunk))

    line_scatter(n, me, part, hold, recv, send, final, s_send, s_recv)
    grad = joined(final)
    _, normed, inverse = norm_apply(xin[...], gain[...], gain[...])
    result = res[...] + norm_back(grad, normed, inverse, gain[...])
    g_ref[...] = result
    small_ref[0:1, :] = jnp.sum(grad * normed, axis=0, keepdims=True)
    small_ref[1:2, :] = jnp.sum(grad, axis=0, keepdims=True)
    small_ref[2:3, :] = jnp.sum(result, axis=0, keepdims=True)
    if not mode:
        return
    all_ref[rows_at(me, rows), :] = result.astype(B16)
    wide = w.shape[0]
    size = STEP_COLS if wide % STEP_COLS == 0 else wide
    if mode == "gelu":
        sum_ref[...] = jnp.zeros_like(sum_ref)
    waited = []

    def on_block(block):
        if not waited:
            w_copy.wait()
            waited.append(True)
        here = rows_at(block, rows)

        def column(i, carry):
            lo = pl.multiple_of(i * size, size)
            value = dot_nt(all_ref[here, :], w[pl.ds(lo, size), :])
            if mode == "gelu":
                value = value * slope[here, pl.ds(lo, size)]
                sum_ref[:, pl.ds(lo, size)] += jnp.sum(value, axis=0, keepdims=True)
            t_ref[here, pl.ds(lo, size)] = value.astype(B16)
            return carry

        lax.fori_loop(0, wide // size, column, 0)

    line_gather(n, me, all_ref, rows, g_send, g_recv, on_block)


def backward_step(lhs, raw, xin, gain, res, collective_id, mode=None, w_all=None, layer=0, slope=None, after=()):
    n = lax.axis_size("group")
    rows, width = res.shape
    ins = [lhs, raw, xin, gain, res]
    specs = [VMEM, ANY, VMEM, VMEM, VMEM]
    outs = [jax.ShapeDtypeStruct((rows, width), F32), jax.ShapeDtypeStruct((8, width), F32)]
    scratch = weight_scratch(raw) + scatter_scratch(n, rows, width)
    us = 21.0
    if mode:
        us = 42.0
        ins.append(w_all)
        specs.append(ANY)
        wide = w_all.shape[1]
        outs += [
            jax.ShapeDtypeStruct((n * rows, width), B16),
            jax.ShapeDtypeStruct((n * rows, wide), B16),
        ]
        scratch += line_sems(n) + [pltpu.VMEM((wide, width), B16), pltpu.SemaphoreType.DMA]
    if mode == "gelu":
        ins.append(slope)
        specs.append(VMEM)
        outs.append(jax.ShapeDtypeStruct((1, wide), F32))
    ins += list(after)
    specs += [ANY] * len(after)
    return pl.pallas_call(
        functools.partial(backward_kernel, n, layer, mode, len(after)),
        out_shape=outs,
        in_specs=specs,
        out_specs=[VMEM] * len(outs),
        scratch_shapes=scratch,
        compiler_params=params(collective_id),
        cost_estimate=cost(us),
        name=f"backward_{mode}_{layer}",
    )(*ins)


def first_kernel(n, normed, x_ref, vec, after, all_ref, g_send, g_recv):
    me = lax.axis_index("group")
    rows = x_ref.shape[0]
    greet_line(n, me)
    value = x_ref[...]
    if normed:
        value = norm_apply(value.astype(F32), vec[0:1, :], vec[1:2, :])[0].astype(B16)
    all_ref[rows_at(me, rows), :] = value
    line_gather(n, me, all_ref, rows, g_send, g_recv, lambda block: None)


def first_gather(x, vec, collective_id, normed, after):
    n = lax.axis_size("group")
    rows, width = x.shape
    return pl.pallas_call(
        functools.partial(first_kernel, n, normed),
        out_shape=jax.ShapeDtypeStruct((n * rows, width), B16),
        in_specs=[VMEM, VMEM, ANY],
        out_specs=VMEM,
        scratch_shapes=line_sems(n),
        compiler_params=params(collective_id),
        cost_estimate=cost(21.0),
        name="first_gather" if normed else "cot_gather",
    )(x, vec, after)


def swap_kernel(n, count, *refs):
    ins, outs = refs[:count], refs[count + 1 : 2 * count + 1]
    send_sems, recv_sems, own_sems = refs[2 * count + 1 :]
    me = lax.axis_index("group")
    peers = [lax.rem(me + step, n) for step in range(1, n)]
    barrier = pltpu.get_barrier_semaphore()
    for peer in peers:
        pl.semaphore_signal(barrier, inc=1, device_id={"group": peer}, device_id_type=MESH)
    pl.semaphore_wait(barrier, n - 1)
    copies = []
    for k in range(count):
        for step, peer in enumerate(peers):
            copy = pltpu.make_async_remote_copy(
                src_ref=ins[k].at[peer],
                dst_ref=outs[k].at[me],
                send_sem=send_sems.at[k, step],
                recv_sem=recv_sems.at[k, step],
                device_id={"group": peer},
                device_id_type=MESH,
            )
            copy.start()
            copies.append(copy)
        own = pltpu.make_async_copy(ins[k].at[me], outs[k].at[me], own_sems.at[k])
        own.start()
        copies.append(own)
    for copy in copies:
        copy.wait()


def weight_swap_kernel(n, jobs, count, *refs):
    piece = refs[len(jobs) + count + 1].shape[1] if jobs else 0
    srcs, plain = refs[: len(jobs)], refs[len(jobs) : len(jobs) + count]
    outs = refs[len(jobs) + count + 1 : 2 * (len(jobs) + count) + 1]
    send_sems, recv_sems, own_sems = refs[2 * (len(jobs) + count) + 1 :]
    me = lax.axis_index("group")
    mine = lax.axis_index("replica")
    peers = [lax.rem(me + step, n) for step in range(1, n)]
    barrier = pltpu.get_barrier_semaphore()
    for peer in peers:
        pl.semaphore_signal(barrier, inc=1, device_id={"group": peer}, device_id_type=MESH)
    pl.semaphore_wait(barrier, n - 1)
    copies = []
    line = [0]

    def move(block, spot):
        for step, peer in enumerate(peers):
            copy = pltpu.make_async_remote_copy(
                src_ref=block(peer),
                dst_ref=spot(me),
                send_sem=send_sems.at[line[0], step],
                recv_sem=recv_sems.at[line[0], step],
                device_id={"group": peer},
                device_id_type=MESH,
            )
            copy.start()
            copies.append(copy)
        own = pltpu.make_async_copy(block(me), spot(me), own_sems.at[line[0]])
        own.start()
        copies.append(own)
        line[0] += 1

    for k in range(count):
        move(lambda i: plain[k].at[i], lambda i: outs[len(jobs) + k].at[i])
    for j, (layer, minor, cols) in enumerate(jobs):
        here = pl.ds(pl.multiple_of(mine * piece, piece), piece)
        for m in range(minor):
            move(
                lambda i: srcs[j].at[layer, here, pl.ds(pl.multiple_of((m * n + i) * cols, 128), cols)],
                lambda i: outs[j].at[i, :, pl.ds(m * cols, cols)],
            )
    for copy in copies:
        copy.wait()


def weight_swap(weights, jobs, plain, collective_id, after, us):
    n, replicas = lax.axis_size("group"), lax.axis_size("replica")
    piece = weights[0].shape[1] // replicas
    lines = sum(job[1] for job in jobs) + len(plain)
    return pl.pallas_call(
        functools.partial(weight_swap_kernel, n, jobs, len(plain)),
        out_shape=[jax.ShapeDtypeStruct((n, piece, job[1] * job[2]), B16) for job in jobs]
        + [jax.ShapeDtypeStruct(b.shape, b.dtype) for b in plain],
        in_specs=[ANY] * len(jobs) + [VMEM] * len(plain) + [ANY],
        out_specs=[VMEM] * (len(jobs) + len(plain)),
        scratch_shapes=[pltpu.SemaphoreType.DMA((lines, n - 1)) for _ in range(2)]
        + [pltpu.SemaphoreType.DMA((lines,))],
        compiler_params=params(collective_id),
        cost_estimate=cost(us),
        name=f"weight_swap_{collective_id}",
    )(*weights, *plain, after)


def swap(blocks, collective_id, after=None, us=8.0):
    n = lax.axis_size("group")
    count = len(blocks)
    return pl.pallas_call(
        functools.partial(swap_kernel, n, count),
        out_shape=[jax.ShapeDtypeStruct(b.shape, b.dtype) for b in blocks],
        in_specs=[VMEM] * count + [ANY],
        out_specs=[VMEM] * count,
        scratch_shapes=[pltpu.SemaphoreType.DMA((count, n - 1)) for _ in range(2)]
        + [pltpu.SemaphoreType.DMA((count,))],
        compiler_params=params(collective_id),
        cost_estimate=cost(us),
        name=f"swap_{collective_id}",
    )(*blocks, blocks[0] if after is None else after)


def grads_kernel(n, a_ref, b_ref, c_ref, d_ref, *refs):
    o_ref, held, sems = refs[-3:]
    own = held.shape[0]
    cols, width = b_ref.shape[1], d_ref.shape[1]
    folds = c_ref.shape[1] // own
    copies = []
    for i in range(n + folds):
        if i < n:
            lo, size = i * cols, cols
            value = dot_tn(a_ref[:, i * own : (i + 1) * own], b_ref[...])
        else:
            lo, size = n * cols + (i - n) * width, width
            value = dot_tn(c_ref[:, (i - n) * own : (i - n + 1) * own], d_ref[...])
        held[:, lo : lo + size] = value.astype(B16)
        copy = pltpu.make_async_copy(
            held.at[:, pl.ds(lo, size)], o_ref.at[:, pl.ds(lo, size)], sems.at[i]
        )
        copy.start()
        copies.append(copy)
    for copy in copies:
        copy.wait()


def grads_pair(a, b, c, d, after=()):
    n = lax.axis_size("group")
    own = a.shape[1] // n
    folds = c.shape[1] // own
    total = n * b.shape[1] + folds * d.shape[1]
    return pl.pallas_call(
        functools.partial(grads_kernel, n),
        out_shape=jax.ShapeDtypeStruct((own, total), B16),
        in_specs=[VMEM] * 4 + [ANY] * len(after),
        out_specs=pl.BlockSpec(memory_space=pltpu.HBM),
        scratch_shapes=[pltpu.VMEM((own, total), B16), pltpu.SemaphoreType.DMA((n + folds,))],
        compiler_params=pltpu.CompilerParams(vmem_limit_bytes=32 * 1024 * 1024),
        cost_estimate=cost(4.0),
        name="weight_grads",
    )(a, b, c, d, *after)


def digit(value, place):
    return (value // 2**place) % 2


def with_digit(value, place, wanted):
    return value + (wanted - digit(value, place)) * 2**place


def flipped(value, place):
    return value + (1 - 2 * digit(value, place)) * 2**place


def exchange_steps(n, cols, minor, src, o_ref, held, sems, reduce):
    replicas = o_ref.shape[0]
    me = lax.axis_index("group")
    mine = lax.axis_index("replica")
    core = digit(mine, 0)
    spot = mine // 2
    halves = replicas // 2
    bits = halves.bit_length() - 1
    total = o_ref.shape[2]
    flow_cols = total // 2
    orders = (list(range(bits)), list(range(bits))[::-1])
    sibling = flipped(mine, 0)
    peers = [lax.rem(me + step, n) for step in range(1, n)]
    landed = held[0]
    swap_send, swap_recv, out_send, out_recv, side_send, side_recv = sems[:6]

    def to_replica(src_ref, dst_ref, send_sem, recv_sem, target):
        copy = pltpu.make_async_remote_copy(
            src_ref=src_ref,
            dst_ref=dst_ref,
            send_sem=send_sem,
            recv_sem=recv_sem,
            device_id={"replica": target},
            device_id_type=MESH,
        )
        copy.start()
        return copy

    def chosen(order, count, index):
        spot_of = spot
        for i in range(count):
            spot_of = with_digit(spot_of, order[i], (index >> i) % 2)
        return spot_of

    sent = []
    if reduce:
        own_half, first_in, acc, flow_in = held[1:]
        pair_send, pair_recv, flow_send, flow_recv, load_sems = sems[6:]
        loads = []
        for q in range(halves):
            load = pltpu.make_async_copy(src.at[2 * q + core], own_half.at[q], load_sems.at[q])
            load.start()
            loads.append(load)
        paired = []
        for q in range(halves):
            paired.append(
                to_replica(
                    src.at[2 * q + 1 - core], first_in.at[q], pair_send.at[q], pair_recv.at[q], sibling
                )
            )
        sent += paired
        yield
        for q in range(halves):
            loads[q].wait()
            paired[q].wait_recv()
            acc[q] = (own_half[q].astype(F32) + first_in[q].astype(F32)).astype(B16)
        slot = 0
        for stage in range(bits):
            started = []
            for flow in (0, 1):
                lanes = pl.ds(flow * flow_cols, flow_cols)
                place = orders[flow][stage]
                free = orders[flow][stage + 1 :]
                for t in range(2 ** len(free)):
                    keep = chosen(free, len(free), t)
                    copy = to_replica(
                        acc.at[flipped(keep, place), :, lanes],
                        flow_in.at[flow, slot + t],
                        flow_send.at[flow, slot + t],
                        flow_recv.at[flow, slot + t],
                        flipped(mine, place + 1),
                    )
                    started.append((copy, flow, slot + t, keep))
            yield
            for copy, flow, at, keep in started:
                copy.wait_recv()
                lanes = slice(flow * flow_cols, (flow + 1) * flow_cols)
                acc[keep, :, lanes] = (
                    acc[keep, :, lanes].astype(F32) + flow_in[flow, at].astype(F32)
                ).astype(B16)
                sent.append(copy)
            slot += 2 ** (bits - 1 - stage)
        whole = acc.at[spot]
    else:
        whole = src

    swaps = []
    for step, peer in enumerate(peers):
        copy = pltpu.make_async_remote_copy(
            src_ref=whole.at[:, pl.ds(pl.multiple_of(peer * cols, 128), cols)],
            dst_ref=landed.at[me],
            send_sem=swap_send.at[step],
            recv_sem=swap_recv.at[step],
            device_id={"group": peer},
            device_id_type=MESH,
        )
        copy.start()
        swaps.append(copy)
    landed[me] = whole[:, pl.ds(pl.multiple_of(me * cols, 128), cols)]
    o_ref[mine, :, n * cols :] = whole[:, n * cols :]
    yield
    for copy in swaps:
        copy.wait_recv()
    sent += swaps
    inner = cols // minor
    for origin in range(n):
        for m in range(minor):
            lo = (m * n + origin) * inner
            o_ref[mine, :, lo : lo + inner] = landed[origin, :, m * inner : (m + 1) * inner]

    def place_out(spot_of, flow):
        return o_ref.at[2 * spot_of + core, :, pl.ds(flow * flow_cols, flow_cols)]

    sides = []

    def to_side(spot_of, flow, index):
        here = place_out(spot_of, flow)
        sides.append(
            to_replica(here, here, side_send.at[flow, index], side_recv.at[flow, index], sibling)
        )

    slot = 0
    for stage in range(bits):
        started = []
        for flow in (0, 1):
            order = orders[flow][::-1]
            place = order[stage]
            for t in range(2**stage):
                here = place_out(chosen(order, stage, t), flow)
                copy = to_replica(
                    here,
                    here,
                    out_send.at[flow, slot + t],
                    out_recv.at[flow, slot + t],
                    flipped(mine, place + 1),
                )
                started.append((copy, flow, t))
        if stage == 0:
            for flow in (0, 1):
                to_side(spot, flow, 0)
        yield
        for copy, flow, t in started:
            order = orders[flow][::-1]
            copy.wait_recv()
            to_side(flipped(chosen(order, stage, t), order[stage]), flow, 2**stage + t)
            sent.append(copy)
        slot += 2**stage
    yield
    for copy in sides:
        copy.wait_recv()
    for copy in sent + sides:
        copy.wait_send()


def exchange_scratch(n, replicas, piece, total, cols, reduce):
    halves = replicas // 2
    dma = lambda *shape: pltpu.SemaphoreType.DMA(shape)
    held = [pltpu.VMEM((n, piece, cols), B16)]
    sems = [dma(n - 1), dma(n - 1)] + [dma(2, halves) for _ in range(4)]
    if reduce:
        held += [pltpu.VMEM((halves, piece, total), B16) for _ in range(3)]
        held.append(pltpu.VMEM((2, halves - 1, piece, total // 2), B16))
        sems += [dma(halves), dma(halves), dma(2, halves), dma(2, halves), dma(halves)]
    return held + sems


def closing_kernel(n, replicas, layer, attn_cols, ffn_cols, *refs):
    refs = list(refs)

    def take(count):
        some = refs[:count]
        del refs[:count]
        return some

    lhs, raw, xin, gain, res, f_lhs, w_any, f_res, bias, attn_src, ffn_src = take(11)
    take(1)
    g_ref, small_ref, y_ref, attn_out, ffn_out = take(5)
    held, h_sems, w, w_sem = take(4)
    line_b, line_f = take(6), take(6)
    attn_held, attn_sems = take(5), take(11)
    ffn_held, ffn_sems = take(1), take(6)
    me = lax.axis_index("group")
    mine = lax.axis_index("replica")
    rows = res.shape[0]
    bits = (replicas // 2).bit_length() - 1
    others = weight_copies(raw, held, h_sems)
    for other in others:
        other.start()
    w_copy = pltpu.make_async_copy(w_any.at[layer], w, w_sem)
    w_copy.start()
    barrier = pltpu.get_barrier_semaphore()
    for place in range(bits + 1):
        pl.semaphore_signal(
            barrier, inc=1, device_id={"replica": flipped(mine, place)}, device_id_type=MESH
        )
    for step in range(1, n):
        pl.semaphore_signal(
            barrier, inc=1, device_id={"group": lax.rem(me + step, n)}, device_id_type=MESH
        )
    pl.semaphore_wait(barrier, bits + n)

    attn = exchange_steps(n, attn_cols, 3, attn_src, attn_out, attn_held, attn_sems, True)
    ffn = exchange_steps(n, ffn_cols, 1, ffn_src, ffn_out, ffn_held, ffn_sems, False)
    next(attn)
    for other in others:
        other.wait()

    def part(block, into):
        own = lhs[rows_at(block, rows), :]
        for chunk in range(CH):
            into[chunk] = dot_nt(own, weight_rows(held, chunk))

    def early(step):
        if step == 0:
            next(attn, None)
            next(ffn, None)
        else:
            next(ffn, None)
        if step == n - 2:
            next(attn, None)

    line_scatter(n, me, part, *line_b, hook=early)
    grad = joined(line_b[3])
    _, normed, inverse = norm_apply(xin[...], gain[...], gain[...])
    result = res[...] + norm_back(grad, normed, inverse, gain[...])
    g_ref[...] = result
    small_ref[0:1, :] = jnp.sum(grad * normed, axis=0, keepdims=True)
    small_ref[1:2, :] = jnp.sum(grad, axis=0, keepdims=True)
    small_ref[2:3, :] = jnp.sum(result, axis=0, keepdims=True)
    next(attn, None)
    w_copy.wait()
    cols = w.shape[1] // CH

    def f_part(block, into):
        own = f_lhs[rows_at(block, rows), :]
        for chunk in range(CH):
            into[chunk] = dot(own, w[:, chunk * cols : (chunk + 1) * cols])

    def late(step):
        next(attn, None)
        if step:
            next(ffn, None)

    line_scatter(n, me, f_part, *line_f, hook=late)
    y_ref[...] = f_res[...] + joined(line_f[3]) + bias[...]
    for steps in (attn, ffn):
        for _ in steps:
            pass


def closing_step(lhs, raw, xin, gain, res, f_lhs, w_all, layer, f_res, bias, attn_grads, ffn_mine, attn_cols, ffn_cols, after):
    n, replicas = lax.axis_size("group"), lax.axis_size("replica")
    rows, width = res.shape
    own, attn_total = attn_grads.shape
    piece, ffn_total = ffn_mine.shape
    full = lambda total: jax.ShapeDtypeStruct((replicas, piece, total), B16)
    flat = jax.ShapeDtypeStruct((rows, width), F32)
    outs = pl.pallas_call(
        functools.partial(closing_kernel, n, replicas, layer, attn_cols, ffn_cols),
        out_shape=[flat, jax.ShapeDtypeStruct((8, width), F32), flat, full(attn_total), full(ffn_total)],
        in_specs=[VMEM, ANY, VMEM, VMEM, VMEM, VMEM, ANY, VMEM, VMEM, ANY, VMEM, ANY],
        out_specs=[VMEM] * 5,
        scratch_shapes=weight_scratch(raw)
        + [pltpu.VMEM(w_all.shape[1:], B16), pltpu.SemaphoreType.DMA]
        + scatter_scratch(n, rows, width)
        + scatter_scratch(n, rows, width)
        + exchange_scratch(n, replicas, piece, attn_total, attn_cols, True)
        + exchange_scratch(n, replicas, piece, ffn_total, ffn_cols, False),
        compiler_params=params(70),
        cost_estimate=cost(50.0),
        name="closing",
    )(
        lhs, raw, xin, gain, res, f_lhs, w_all, f_res, bias,
        attn_grads.reshape(replicas, piece, attn_total), ffn_mine, after,
    )
    g, small, y, attn_full, ffn_full = outs
    return g, small, y, attn_full.reshape(own, attn_total), ffn_full.reshape(own, ffn_total)


def small_sums_kernel(n, replicas, wide, ups, o_ref, landed, both, spread, *sems):
    a_send, a_recv, b_send, b_recv = sems
    me = lax.axis_index("group")
    mine = lax.axis_index("replica")
    rows = landed.shape[1]
    peers = [lax.rem(me + step, n) for step in range(1, n)]
    mates = [lax.rem(mine + step, replicas) for step in range(1, replicas)]
    barrier = pltpu.get_barrier_semaphore()
    for peer in peers:
        pl.semaphore_signal(barrier, inc=1, device_id={"group": peer}, device_id_type=MESH)
    for mate in mates:
        pl.semaphore_signal(barrier, inc=1, device_id={"replica": mate}, device_id_type=MESH)
    pl.semaphore_wait(barrier, n + replicas - 2)
    copies = []
    for step, peer in enumerate(peers):
        copy = pltpu.make_async_remote_copy(
            src_ref=wide.at[peer],
            dst_ref=landed.at[me],
            send_sem=a_send.at[step],
            recv_sem=a_recv.at[step],
            device_id={"group": peer},
            device_id_type=MESH,
        )
        copy.start()
        copies.append(copy)
    landed[me] = wide[me]
    for copy in copies:
        copy.wait_recv()
    total = landed[0]
    for i in range(1, n):
        total = total + landed[i]
    both[0:rows, :] = total
    both[rows:, :] = ups[...]
    spread[mine] = both[...]
    others = []
    for step, mate in enumerate(mates):
        copy = pltpu.make_async_remote_copy(
            src_ref=both,
            dst_ref=spread.at[mine],
            send_sem=b_send.at[step],
            recv_sem=b_recv.at[step],
            device_id={"replica": mate},
            device_id_type=MESH,
        )
        copy.start()
        others.append(copy)
    for copy in others:
        copy.wait_recv()
    total = spread[0]
    for i in range(1, replicas):
        total = total + spread[i]
    o_ref[...] = total
    for copy in copies + others:
        copy.wait_send()


def small_sums(wide, ups, collective_id):
    n, replicas = lax.axis_size("group"), lax.axis_size("replica")
    _, rows, own = wide.shape
    lines = rows + ups.shape[0]
    return pl.pallas_call(
        functools.partial(small_sums_kernel, n, replicas),
        out_shape=jax.ShapeDtypeStruct((lines, own), F32),
        in_specs=[VMEM, VMEM],
        out_specs=VMEM,
        scratch_shapes=[
            pltpu.VMEM((n, rows, own), F32),
            pltpu.VMEM((lines, own), F32),
            pltpu.VMEM((replicas, lines, own), F32),
            pltpu.SemaphoreType.DMA((n - 1,)),
            pltpu.SemaphoreType.DMA((n - 1,)),
            pltpu.SemaphoreType.DMA((replicas - 1,)),
            pltpu.SemaphoreType.DMA((replicas - 1,)),
        ],
        compiler_params=params(collective_id),
        cost_estimate=cost(9.0),
        name="small_sums",
    )(wide, ups)


def widen_kernel(lead, *refs):
    full, cols_out, rows_out = refs[0], refs[-2], refs[-1]
    step = pl.program_id(0)

    @pl.when(step < lead)
    def _():
        cols_out[0] = full[...].astype(F32)

    @pl.when(step >= lead)
    def _():
        rows_out[0] = full[...].astype(F32)


def widen(full, cut, width, layer, layers, before):
    own, total = full.shape
    lead, folds = cut // width, (total - cut) // width
    block = (1, own, width)
    return pl.pallas_call(
        functools.partial(widen_kernel, lead),
        grid=(lead + folds,),
        out_shape=[
            jax.ShapeDtypeStruct((layers, own, cut), F32),
            jax.ShapeDtypeStruct((layers, own * folds, width), F32),
        ],
        in_specs=[pl.BlockSpec((own, width), lambda j: (0, j))] + [ANY] * len(before),
        out_specs=[
            pl.BlockSpec(block, lambda j: (layer, 0, jnp.minimum(j, lead - 1))),
            pl.BlockSpec(block, lambda j: (layer, jnp.maximum(j - lead, 0), 0)),
        ],
        input_output_aliases={1: 0, 2: 1} if before else {},
        compiler_params=pltpu.CompilerParams(vmem_limit_bytes=24 * 1024 * 1024),
        cost_estimate=cost(own * total * 6 / 3.3e6),
        name=f"widen_{layer}",
    )(full, *before)


def attention(q, k, v, first_head, heads_here):
    tokens = q.shape[0]
    split = lambda m: m.reshape(tokens, heads_here, HEAD_DIM).transpose(1, 0, 2)
    q, k, v = split(q), split(k), split(v)
    head_ids = (first_head + jnp.arange(heads_here, dtype=jnp.int32)).astype(F32)
    slopes = 2.0 ** (-8.0 * (head_ids + 1.0) / HEADS)
    pos = jnp.arange(tokens, dtype=jnp.int32)
    offset = (pos[:, None] - pos[None, :]).astype(F32)
    raw = jnp.einsum("hqd,hkd->hqk", q, k, preferred_element_type=F32)
    scores = raw * HEAD_DIM ** (-0.5) - slopes[:, None, None] * offset[None]
    scores = jnp.where((offset >= 0.0)[None], scores, NEG)
    row_top = jnp.max(scores, axis=-1, keepdims=True)
    exps_raw = jnp.exp(scores - row_top)
    row_total = jnp.sum(exps_raw, axis=-1, keepdims=True)
    probs = (exps_raw * (1.0 / row_total)).astype(B16)
    context = jnp.einsum("hqk,hkd->hqd", probs, v, preferred_element_type=F32).astype(B16)
    return context.transpose(1, 0, 2).reshape(tokens, -1), (q, k, v, probs, context)


def attention_back(d_context, saved):
    q, k, v, probs, context = saved
    heads_here, tokens, _ = q.shape
    dc = d_context.reshape(tokens, heads_here, HEAD_DIM).transpose(1, 0, 2)
    d_probs = jnp.einsum("hqd,hkd->hqk", dc, v, preferred_element_type=F32)
    delta = jnp.sum(dc.astype(F32) * context.astype(F32), axis=-1, keepdims=True)
    ds = (probs.astype(F32) * (d_probs - delta)).astype(B16)
    scale = HEAD_DIM ** (-0.5)
    dq = jnp.einsum("hqk,hkd->hqd", ds, k, preferred_element_type=F32) * scale
    dk = jnp.einsum("hqk,hqd->hkd", ds, q, preferred_element_type=F32) * scale
    dv = jnp.einsum("hqk,hqd->hkd", probs, dc, preferred_element_type=F32)
    sums = (jnp.sum(dq, axis=1).reshape(-1), jnp.sum(dv, axis=1).reshape(-1))
    join = lambda m: m.astype(B16).transpose(1, 0, 2).reshape(tokens, -1)
    return jnp.concatenate([join(dq), join(dk), join(dv)], axis=1), sums


def local(
    inputs,
    cotangent,
    norm_gain,
    norm_bias,
    w_qkv,
    bias_qv,
    w_out,
    bias_out,
    w_up,
    bias_up,
    w_down,
    bias_down,
):
    groups = lax.axis_size("group")
    replicas = lax.axis_size("replica")
    me = lax.axis_index("group")
    copy_idx = lax.axis_index("replica")
    layers, own, _ = w_qkv.shape
    width = own * groups
    ff_own = w_down.shape[1]
    heads_here = HEADS // groups
    piece = own // replicas

    def share(block):
        full = lax.all_gather(block, "replica", axis=0)
        if piece % 16:
            full = full.transpose(1, 0, 2, 3).reshape(1, 1, width, -1)
        return full

    small = jnp.concatenate(
        [norm_gain, norm_bias, bias_qv.reshape(layers, 2, own), bias_out[:, None], bias_down[:, None]],
        axis=1,
    ).reshape(layers * 8, own)
    small = jnp.broadcast_to(small[None], (groups,) + small.shape)
    wq_first, small = weight_swap([w_qkv], [(0, 3, own)], [small], 0, bias_up, 9.0)
    wq = [share(wq_first)] + [None] * (layers - 1)
    wu = [None] * layers

    small = small.reshape(groups, layers, 8, own).astype(F32)
    rows_of = lambda i: small[:, :, i].transpose(1, 0, 2).reshape(layers, width)
    gains = [rows_of(0), rows_of(1)]
    shifts = [rows_of(2), rows_of(3)]
    qv_full = small[:, :, 4:6].transpose(1, 0, 2, 3).reshape(layers, 2 * width)
    q_bias = lax.dynamic_slice_in_dim(qv_full, me * own, own, axis=1)
    v_bias = lax.dynamic_slice_in_dim(qv_full, width + me * own, own, axis=1)
    qkv_bias = jnp.concatenate([q_bias, jnp.zeros_like(q_bias), v_bias], axis=1)
    out_bias, down_bias = rows_of(6), rows_of(7)
    up_bias = bias_up.astype(F32)

    x = inputs[0].astype(F32)
    vec0 = jnp.stack([gains[0][0], shifts[0][0]])
    a1_all = first_gather(inputs[0], vec0, 1, True, wq_first)
    jobs = [(l, 1, ff_own) for l in range(layers)] + [(l, 3, own) for l in range(1, layers)]
    later = weight_swap([w_up] * layers + [w_qkv] * (layers - 1), jobs, [], 2, a1_all, 18.0)
    for l in range(layers):
        wu[l] = share(later[l])
        if l:
            wq[l] = share(later[layers + l - 1])
    cot_all = first_gather(cotangent[0], vec0, 3, False, later[0])

    full0 = wq[0].transpose(1, 0, 2, 3).reshape(width, 3 * own)
    proj = (dot(a1_all, full0) + qkv_bias[0]).astype(B16)
    kept = []
    for l in range(layers):
        cut = lambda i: proj[:, i * own : (i + 1) * own]
        context, attn_saved = attention(cut(0), cut(1), cut(2), me * heads_here, heads_here)
        vec = jnp.stack([out_bias[l], gains[1][l], shifts[1][l]])
        h, a2_all, hidden, slope = forward_step(
            context, w_out, l, x, vec, 10 + 4 * l, "gelu", wu[l], up_bias[l][None]
        )
        saved = (x, a1_all, attn_saved, context, h, a2_all, slope, hidden)
        if l + 1 < layers:
            vec = jnp.stack([down_bias[l], gains[0][l + 1], shifts[0][l + 1]])
            x, a1_all, proj = forward_step(
                hidden, w_down, l, h, vec, 11 + 4 * l, "bias", wq[l + 1], qkv_bias[l + 1][None]
            )
        kept.append(saved)

    def reduce_pair(grads):
        return lax.psum_scatter(grads, "replica", scatter_dimension=0, tiled=True)

    def swap_pair(mine, cols, collective_id, after=None):
        cut = groups * cols
        left = mine[:, :cut].reshape(piece, groups, cols).transpose(1, 0, 2)
        return swap([left], collective_id, after)[0]

    def share_pair(left, mine, cols, minor):
        cut = groups * cols
        left = left.reshape(groups, piece, minor, cols // minor).transpose(1, 2, 0, 3)
        mine = jnp.concatenate([left.reshape(piece, cut), mine[:, cut:]], axis=1)
        return lax.all_gather(mine, "replica", axis=0, tiled=True)

    g = cotangent[0].astype(F32)
    g_sum = jnp.sum(g, axis=0)
    g_all = cot_all
    smalls = [None] * layers
    ffn_sum = [None] * layers
    attn_sum = [None] * layers
    ffn_full = [None] * layers
    attn_full = [None] * layers
    zeros_qv = jnp.zeros((2 * width,), F32)
    pre = up_sum = None
    waits = ()
    for l in reversed(range(layers)):
        x_in, a1_all, attn_saved, context, h, a2_all, slope, hidden = kept[l]
        if pre is None:
            d_pre = dot_nt(g_all, w_down[l]) * slope
            up_sum = jnp.sum(d_pre, axis=0)
            pre = d_pre.astype(B16)
        ffn_grads = grads_pair(a2_all, pre, hidden, g_all)
        ffn_sum[l] = reduce_pair(ffn_grads)
        down_sum, ups = g_sum, up_sum
        dh, small1, dh_all, dc = backward_step(
            pre, wu[l], h, gains[1][l][None], g, 30 + 4 * l, "plain", w_out, l, after=(ffn_grads,) + waits
        )
        d_proj, (dq_sum, dv_sum) = attention_back(dc, attn_saved)
        attn_grads = grads_pair(a1_all, d_proj, context, dh_all, (ffn_sum[l],) if l else ())
        if l:
            attn_sum[l] = reduce_pair(attn_grads)
            ffn_left = swap_pair(ffn_sum[l], ff_own, 60 + 4 * l, attn_grads)
            ffn_full[l] = share_pair(ffn_left, ffn_sum[l], ff_own, 1)
            g, small0, g_all, pre, up_sum = backward_step(
                d_proj, wq[l], x_in, gains[0][l][None], dh, 31 + 4 * l, "gelu", w_down, l - 1, kept[l - 1][6],
                after=(attn_grads, ffn_left),
            )
            attn_left = swap_pair(attn_sum[l], 3 * own, 61 + 4 * l, small0)
            attn_full[l] = share_pair(attn_left, attn_sum[l], 3 * own, 3)
            waits = (attn_left,)
            g_sum, up_sum = small0[2], up_sum[0]
        else:
            last = kept[layers - 1]
            g, small0, x, attn_full[l], ffn_full[l] = closing_step(
                d_proj, wq[l], x_in, gains[0][l][None], dh, last[7], w_down, layers - 1, last[4],
                down_bias[layers - 1][None], attn_grads, ffn_sum[l], 3 * own, ff_own, attn_grads,
            )
            outputs = x.astype(B16)[None]
        qv = lax.dynamic_update_slice_in_dim(zeros_qv, dq_sum, me * own, axis=0)
        qv = lax.dynamic_update_slice_in_dim(qv, dv_sum, width + me * own, axis=0)
        smalls[l] = (
            jnp.concatenate([small0[0], small1[0], small0[1], small1[1], qv, small1[2], down_sum]),
            ups,
        )

    ffn_out, attn_out = (), ()
    for l in reversed(range(layers)):
        ffn_out = tuple(widen(ffn_full[l], groups * ff_own, width, l, layers, ffn_out))
        attn_out = tuple(widen(attn_full[l], 3 * width, width, l, layers, attn_out))

    wide = jnp.stack([s[0] for s in smalls])
    per_owner = lambda lo, n: wide[:, lo * width : (lo + n) * width].reshape(layers, n, groups, own)
    gain_bias = per_owner(0, 4).transpose(2, 0, 1, 3)
    qv = wide[:, 4 * width : 6 * width].reshape(layers, groups, 2, own).transpose(1, 0, 2, 3)
    dense = per_owner(6, 2).transpose(2, 0, 1, 3)
    wide = jnp.concatenate([gain_bias, qv, dense], axis=2)
    ups = jnp.stack([s[1] for s in smalls]).reshape(-1, own)
    total = small_sums(wide.reshape(groups, layers * 8, own), ups, 5)
    own_cols = total[: layers * 8].reshape(layers, 8, own)
    up_total = total[layers * 8 :].reshape(layers, ff_own)
    qv_total = own_cols[:, 4:6].reshape(layers, 2 * own)
    return (
        outputs,
        g[None],
        own_cols[:, 0:2],
        own_cols[:, 2:4],
        attn_out[0],
        qv_total,
        attn_out[1],
        own_cols[:, 6],
        ffn_out[0],
        up_total,
        ffn_out[1],
        own_cols[:, 7],
    )


def solution(mesh):
    rows = P("replica", "group", None)
    vec = P(None, None, "group")
    mat = P(None, "group", None)
    bias = P(None, "group")
    params_in = (vec, vec, mat, bias, mat, bias, mat, bias, mat, bias)
    return jax.shard_map(
        local,
        mesh=mesh,
        in_specs=(rows, rows) + params_in,
        out_specs=(rows, rows) + params_in,
        check_vma=False,
    )
```

```python
import functools

import jax
import jax.numpy as jnp
from jax import lax
from jax.experimental import pallas as pl
from jax.experimental.pallas import tpu as pltpu
from jax.sharding import PartitionSpec as P

HEADS = 16
HEAD_DIM = 64

EPS = 1e-05
NEG = -1e30
GELU_C = 0.7978845608028654
GELU_A = 0.044715
F32 = jnp.float32
B16 = jnp.bfloat16
MESH = pl.DeviceIdType.MESH
CH = 4

VMEM = pl.BlockSpec(memory_space=pltpu.VMEM)
ANY = pl.BlockSpec(memory_space=pl.ANY)


def norm_apply(values_in, gain_row, bias_row):
    row_mean = jnp.mean(values_in, axis=-1, keepdims=True)
    centered = values_in - row_mean
    variance = jnp.mean(centered * centered, axis=-1, keepdims=True)
    inverse = lax.rsqrt(variance + EPS)
    normed = centered * inverse
    return (normed * gain_row + bias_row, normed, inverse)


def norm_back(grad_in, normed, inverse, gain_row):
    scaled = grad_in * gain_row
    return inverse * (
        scaled
        - jnp.mean(scaled, axis=-1, keepdims=True)
        - normed * jnp.mean(scaled * normed, axis=-1, keepdims=True)
    )


def gelu_parts(pre_act):
    tanh_val = jnp.tanh(GELU_C * (pre_act + GELU_A * pre_act * pre_act * pre_act))
    gelu_value = 0.5 * pre_act * (1.0 + tanh_val)
    gelu_slope = 0.5 * (1.0 + tanh_val) + 0.5 * pre_act * (1.0 - tanh_val * tanh_val) * GELU_C * (
        1.0 + 3.0 * GELU_A * pre_act * pre_act
    )
    return (gelu_value, gelu_slope)


def dot(a, b):
    return jnp.dot(a, b, preferred_element_type=F32)


def dot_nt(a, b):
    return lax.dot_general(a, b, (((1,), (1,)), ((), ())), preferred_element_type=F32)


def dot_tn(a, b):
    return lax.dot_general(a, b, (((0,), (0,)), ((), ())), preferred_element_type=F32)


def greet_line(n, me):
    barrier = pltpu.get_barrier_semaphore()
    for there, peer in ((me > 0, me - 1), (me < n - 1, me + 1)):

        @pl.when(there)
        def _():
            pl.semaphore_signal(barrier, inc=1, device_id={"group": peer}, device_id_type=MESH)

    beside_me = (me > 0).astype(jnp.int32) + (me < n - 1).astype(jnp.int32)
    pl.semaphore_wait(barrier, beside_me)


def beside(way, me):
    return me + 1 if way == 0 else me - 1


def line_gather(n, me, buf, rows, send_sems, recv_sems, on_block):
    part = rows // CH

    def copy(way, step, chunk, block):
        here = pl.ds(pl.multiple_of(block * rows + chunk * part, part), part)
        return pltpu.make_async_remote_copy(
            src_ref=buf.at[here],
            dst_ref=buf.at[here],
            send_sem=send_sems.at[way, step, chunk],
            recv_sem=recv_sems.at[way, step, chunk],
            device_id={"group": beside(way, me)},
            device_id_type=MESH,
        )

    def block_of(way, step):
        return me - step if way == 0 else me + step

    def have(way, step):
        return me - step >= 0 if way == 0 else me + step < n

    def onward(way):
        return me < n - 1 if way == 0 else me > 0

    for chunk in range(CH):
        for way in (0, 1):

            @pl.when(onward(way))
            def _():
                copy(way, 0, chunk, me).start()

    on_block(me)

    def advance(step, carry):
        for chunk in range(CH):
            for way in (0, 1):

                @pl.when(have(way, step))
                def _():
                    copy(way, step - 1, chunk, block_of(way, step)).wait_recv()

                @pl.when(have(way, step) & onward(way) & (step < n - 1))
                def _():
                    copy(way, step, chunk, block_of(way, step)).start()

        for way in (0, 1):

            @pl.when(have(way, step))
            def _():
                on_block(block_of(way, step))

        return carry

    lax.fori_loop(1, n, advance, 0)

    def drain(step, carry):
        for way in (0, 1):

            @pl.when(have(way, step) & onward(way))
            def _():
                for chunk in range(CH):
                    copy(way, step, chunk, block_of(way, step)).wait_send()

        return carry

    lax.fori_loop(0, n - 1, drain, 0)


def line_scatter(n, me, part, hold, recv, send, final, send_sems, recv_sems, hook=None):
    def copy(way, step, chunk):
        return pltpu.make_async_remote_copy(
            src_ref=send.at[way, step, chunk],
            dst_ref=recv.at[way, step, chunk],
            send_sem=send_sems.at[way, step, chunk],
            recv_sem=recv_sems.at[way, step, chunk],
            device_id={"group": beside(way, me)},
            device_id_type=MESH,
        )

    def goal(way, step):
        return n - 1 - step if way == 0 else step

    def onward(way, step):
        return goal(way, step) > me if way == 0 else goal(way, step) < me

    def fed(way):
        return me > 0 if way == 0 else me < n - 1

    def advance(step, carry):
        for way in (0, 1):
            on = onward(way, step)

            @pl.when(on)
            def _():
                part(goal(way, step), hold)
                for chunk in range(CH):

                    @pl.when(fed(way))
                    def _():
                        copy(way, step, chunk).wait_recv()
                        send[way, step, chunk] = (hold[chunk] + recv[way, step, chunk].astype(F32)).astype(B16)

                    @pl.when(jnp.logical_not(fed(way)))
                    def _():
                        send[way, step, chunk] = hold[chunk].astype(B16)

                    copy(way, step, chunk).start()

        return carry

    if hook is None:
        lax.fori_loop(0, n - 1, advance, 0)
    else:
        for step in range(n - 1):
            advance(step, 0)
            hook(step)
    part(me, final)

    def collect(step, carry):
        for way in (0, 1):

            @pl.when((goal(way, step) == me) & fed(way))
            def _():
                for chunk in range(CH):
                    copy(way, step, chunk).wait_recv()
                    final[chunk] = final[chunk] + recv[way, step, chunk].astype(F32)

            @pl.when(onward(way, step))
            def _():
                for chunk in range(CH):
                    copy(way, step, chunk).wait_send()

        return carry

    lax.fori_loop(0, n - 1, collect, 0)


def line_sems(n):
    return [pltpu.SemaphoreType.DMA((2, n - 1, CH)) for _ in range(2)]


def scatter_scratch(n, rows, width):
    cols = width // CH
    return [
        pltpu.VMEM((CH, rows, cols), F32),
        pltpu.VMEM((2, n - 1, CH, rows, cols), B16),
        pltpu.VMEM((2, n - 1, CH, rows, cols), B16),
        pltpu.VMEM((CH, rows, cols), F32),
    ] + line_sems(n)


def rows_at(block, rows):
    return pl.ds(pl.multiple_of(block * rows, rows), rows)


def joined(final):
    return jnp.concatenate([final[chunk] for chunk in range(CH)], axis=1)


def weight_scratch(raw):
    outer, inner, piece, cols = raw.shape
    return [pltpu.VMEM((inner, outer, piece, cols), raw.dtype), pltpu.SemaphoreType.DMA((inner,))]


def weight_copies(raw, held, sems):
    return [
        pltpu.make_async_copy(raw.at[:, i], held.at[i], sems.at[i]) for i in range(held.shape[0])
    ]


def weight_cols(held, lo, size):
    inner, outer, piece, _ = held.shape
    return held[:, :, :, pl.ds(lo, size)].reshape(inner * outer * piece, size)


def weight_rows(held, chunk):
    inner, outer, piece, cols = held.shape
    if inner % CH == 0:
        take = inner // CH
        return held[chunk * take : (chunk + 1) * take].reshape(take * outer * piece, cols)
    take = piece // CH
    return held[0, 0, chunk * take : (chunk + 1) * take, :]


def params(collective_id):
    return pltpu.CompilerParams(
        collective_id=collective_id, has_side_effects=True, vmem_limit_bytes=48 * 1024 * 1024
    )


def cost(us):
    return pl.CostEstimate(flops=0, bytes_accessed=int(us * 3.3e6), transcendentals=0)


STEP_COLS = 256


def forward_kernel(n, layer, mode, waits, *refs):
    refs = list(refs)
    lhs, w_any, res, vec = refs[:4]
    del refs[:4]
    raw = bias = None
    if mode:
        raw, bias = refs[:2]
        del refs[:2]
    del refs[:waits]
    y_ref = refs.pop(0)
    outs = []
    if mode:
        count = 3 if mode == "gelu" else 2
        outs = refs[:count]
        del refs[:count]
    w, w_sem, hold, recv, send, final, s_send, s_recv = refs[:8]
    del refs[:8]
    me = lax.axis_index("group")
    rows = res.shape[0]
    w_copy = pltpu.make_async_copy(w_any.at[layer], w, w_sem)
    w_copy.start()
    if mode:
        g_send, g_recv, held, h_sems = refs
        others = weight_copies(raw, held, h_sems)
        for other in others:
            other.start()
    greet_line(n, me)
    w_copy.wait()
    cols = w.shape[1] // CH

    def part(block, into):
        mine = lhs[rows_at(block, rows), :]
        for chunk in range(CH):
            into[chunk] = dot(mine, w[:, chunk * cols : (chunk + 1) * cols])

    line_scatter(n, me, part, hold, recv, send, final, s_send, s_recv)
    y = res[...] + joined(final) + vec[0:1, :]
    y_ref[...] = y
    if not mode:
        return
    all_ref = outs[0]
    all_ref[rows_at(me, rows), :] = norm_apply(y, vec[1:2, :], vec[2:3, :])[0].astype(B16)
    wide = held.shape[-1]
    size = STEP_COLS if wide % STEP_COLS == 0 else wide
    waited = []

    def on_block(block):
        if not waited:
            for other in others:
                other.wait()
            waited.append(True)
        here = rows_at(block, rows)

        def column(i, carry):
            lo = pl.multiple_of(i * size, size)
            value = dot(all_ref[here, :], weight_cols(held, lo, size)) + bias[:, pl.ds(lo, size)]
            if mode == "gelu":
                value, slope = gelu_parts(value)
                outs[2][here, pl.ds(lo, size)] = slope
            outs[1][here, pl.ds(lo, size)] = value.astype(B16)
            return carry

        lax.fori_loop(0, wide // size, column, 0)

    line_gather(n, me, all_ref, rows, g_send, g_recv, on_block)


def forward_step(lhs, w_all, layer, res, vec, collective_id, mode=None, raw=None, bias=None, after=()):
    n = lax.axis_size("group")
    rows, width = res.shape
    depth = w_all.shape[1]
    ins = [lhs, w_all, res, vec]
    specs = [VMEM, ANY, VMEM, VMEM]
    outs = [jax.ShapeDtypeStruct((rows, width), F32)]
    scratch = [pltpu.VMEM((depth, width), B16), pltpu.SemaphoreType.DMA] + scatter_scratch(n, rows, width)
    us = 21.0
    if mode:
        us = 42.0
        ins += [raw, bias]
        specs += [ANY, VMEM]
        wide = raw.shape[-1]
        outs += [
            jax.ShapeDtypeStruct((n * rows, width), B16),
            jax.ShapeDtypeStruct((n * rows, wide), B16),
        ]
        if mode == "gelu":
            outs.append(jax.ShapeDtypeStruct((n * rows, wide), F32))
        scratch += line_sems(n) + weight_scratch(raw)
    ins += list(after)
    specs += [ANY] * len(after)
    return pl.pallas_call(
        functools.partial(forward_kernel, n, layer, mode, len(after)),
        out_shape=outs,
        in_specs=specs,
        out_specs=[VMEM] * len(outs),
        scratch_shapes=scratch,
        compiler_params=params(collective_id),
        cost_estimate=cost(us),
        name=f"forward_{mode}_{layer}",
    )(*ins)


def backward_kernel(n, layer, mode, waits, *refs):
    refs = list(refs)
    lhs, raw, xin, gain, res = refs[:5]
    del refs[:5]
    if mode:
        w_any = refs.pop(0)
    if mode == "gelu":
        slope = refs.pop(0)
    del refs[:waits]
    g_ref, small_ref = refs[:2]
    del refs[:2]
    if mode:
        all_ref, t_ref = refs[:2]
        del refs[:2]
    if mode == "gelu":
        sum_ref = refs.pop(0)
    held, h_sems, hold, recv, send, final, s_send, s_recv = refs[:8]
    del refs[:8]
    me = lax.axis_index("group")
    rows = res.shape[0]
    others = weight_copies(raw, held, h_sems)
    for other in others:
        other.start()
    if mode:
        g_send, g_recv, w, w_sem = refs
        w_copy = pltpu.make_async_copy(w_any.at[layer], w, w_sem)
        w_copy.start()
    greet_line(n, me)
    for other in others:
        other.wait()

    def part(block, into):
        mine = lhs[rows_at(block, rows), :]
        for chunk in range(CH):
            into[chunk] = dot_nt(mine, weight_rows(held, chunk))

    line_scatter(n, me, part, hold, recv, send, final, s_send, s_recv)
    grad = joined(final)
    _, normed, inverse = norm_apply(xin[...], gain[...], gain[...])
    result = res[...] + norm_back(grad, normed, inverse, gain[...])
    g_ref[...] = result
    small_ref[0:1, :] = jnp.sum(grad * normed, axis=0, keepdims=True)
    small_ref[1:2, :] = jnp.sum(grad, axis=0, keepdims=True)
    small_ref[2:3, :] = jnp.sum(result, axis=0, keepdims=True)
    if not mode:
        return
    all_ref[rows_at(me, rows), :] = result.astype(B16)
    wide = w.shape[0]
    size = STEP_COLS if wide % STEP_COLS == 0 else wide
    if mode == "gelu":
        sum_ref[...] = jnp.zeros_like(sum_ref)
    waited = []

    def on_block(block):
        if not waited:
            w_copy.wait()
            waited.append(True)
        here = rows_at(block, rows)

        def column(i, carry):
            lo = pl.multiple_of(i * size, size)
            value = dot_nt(all_ref[here, :], w[pl.ds(lo, size), :])
            if mode == "gelu":
                value = value * slope[here, pl.ds(lo, size)]
                sum_ref[:, pl.ds(lo, size)] += jnp.sum(value, axis=0, keepdims=True)
            t_ref[here, pl.ds(lo, size)] = value.astype(B16)
            return carry

        lax.fori_loop(0, wide // size, column, 0)

    line_gather(n, me, all_ref, rows, g_send, g_recv, on_block)


def backward_step(lhs, raw, xin, gain, res, collective_id, mode=None, w_all=None, layer=0, slope=None, after=()):
    n = lax.axis_size("group")
    rows, width = res.shape
    ins = [lhs, raw, xin, gain, res]
    specs = [VMEM, ANY, VMEM, VMEM, VMEM]
    outs = [jax.ShapeDtypeStruct((rows, width), F32), jax.ShapeDtypeStruct((8, width), F32)]
    scratch = weight_scratch(raw) + scatter_scratch(n, rows, width)
    us = 21.0
    if mode:
        us = 42.0
        ins.append(w_all)
        specs.append(ANY)
        wide = w_all.shape[1]
        outs += [
            jax.ShapeDtypeStruct((n * rows, width), B16),
            jax.ShapeDtypeStruct((n * rows, wide), B16),
        ]
        scratch += line_sems(n) + [pltpu.VMEM((wide, width), B16), pltpu.SemaphoreType.DMA]
    if mode == "gelu":
        ins.append(slope)
        specs.append(VMEM)
        outs.append(jax.ShapeDtypeStruct((1, wide), F32))
    ins += list(after)
    specs += [ANY] * len(after)
    return pl.pallas_call(
        functools.partial(backward_kernel, n, layer, mode, len(after)),
        out_shape=outs,
        in_specs=specs,
        out_specs=[VMEM] * len(outs),
        scratch_shapes=scratch,
        compiler_params=params(collective_id),
        cost_estimate=cost(us),
        name=f"backward_{mode}_{layer}",
    )(*ins)


def first_kernel(n, normed, x_ref, vec, after, all_ref, g_send, g_recv):
    me = lax.axis_index("group")
    rows = x_ref.shape[0]
    greet_line(n, me)
    value = x_ref[...]
    if normed:
        value = norm_apply(value.astype(F32), vec[0:1, :], vec[1:2, :])[0].astype(B16)
    all_ref[rows_at(me, rows), :] = value
    line_gather(n, me, all_ref, rows, g_send, g_recv, lambda block: None)


def first_gather(x, vec, collective_id, normed, after):
    n = lax.axis_size("group")
    rows, width = x.shape
    return pl.pallas_call(
        functools.partial(first_kernel, n, normed),
        out_shape=jax.ShapeDtypeStruct((n * rows, width), B16),
        in_specs=[VMEM, VMEM, ANY],
        out_specs=VMEM,
        scratch_shapes=line_sems(n),
        compiler_params=params(collective_id),
        cost_estimate=cost(21.0),
        name="first_gather" if normed else "cot_gather",
    )(x, vec, after)


def swap_kernel(n, count, *refs):
    ins, outs = refs[:count], refs[count + 1 : 2 * count + 1]
    send_sems, recv_sems, own_sems = refs[2 * count + 1 :]
    me = lax.axis_index("group")
    peers = [lax.rem(me + step, n) for step in range(1, n)]
    barrier = pltpu.get_barrier_semaphore()
    for peer in peers:
        pl.semaphore_signal(barrier, inc=1, device_id={"group": peer}, device_id_type=MESH)
    pl.semaphore_wait(barrier, n - 1)
    copies = []
    for k in range(count):
        for step, peer in enumerate(peers):
            copy = pltpu.make_async_remote_copy(
                src_ref=ins[k].at[peer],
                dst_ref=outs[k].at[me],
                send_sem=send_sems.at[k, step],
                recv_sem=recv_sems.at[k, step],
                device_id={"group": peer},
                device_id_type=MESH,
            )
            copy.start()
            copies.append(copy)
        own = pltpu.make_async_copy(ins[k].at[me], outs[k].at[me], own_sems.at[k])
        own.start()
        copies.append(own)
    for copy in copies:
        copy.wait()


def weight_swap_kernel(n, jobs, count, *refs):
    piece = refs[len(jobs) + count + 1].shape[1] if jobs else 0
    srcs, plain = refs[: len(jobs)], refs[len(jobs) : len(jobs) + count]
    outs = refs[len(jobs) + count + 1 : 2 * (len(jobs) + count) + 1]
    send_sems, recv_sems, own_sems = refs[2 * (len(jobs) + count) + 1 :]
    me = lax.axis_index("group")
    mine = lax.axis_index("replica")
    peers = [lax.rem(me + step, n) for step in range(1, n)]
    barrier = pltpu.get_barrier_semaphore()
    for peer in peers:
        pl.semaphore_signal(barrier, inc=1, device_id={"group": peer}, device_id_type=MESH)
    pl.semaphore_wait(barrier, n - 1)
    copies = []
    line = [0]

    def move(block, spot):
        for step, peer in enumerate(peers):
            copy = pltpu.make_async_remote_copy(
                src_ref=block(peer),
                dst_ref=spot(me),
                send_sem=send_sems.at[line[0], step],
                recv_sem=recv_sems.at[line[0], step],
                device_id={"group": peer},
                device_id_type=MESH,
            )
            copy.start()
            copies.append(copy)
        own = pltpu.make_async_copy(block(me), spot(me), own_sems.at[line[0]])
        own.start()
        copies.append(own)
        line[0] += 1

    for k in range(count):
        move(lambda i: plain[k].at[i], lambda i: outs[len(jobs) + k].at[i])
    for j, (layer, minor, cols) in enumerate(jobs):
        here = pl.ds(pl.multiple_of(mine * piece, piece), piece)
        for m in range(minor):
            move(
                lambda i: srcs[j].at[layer, here, pl.ds(pl.multiple_of((m * n + i) * cols, 128), cols)],
                lambda i: outs[j].at[i, :, pl.ds(m * cols, cols)],
            )
    for copy in copies:
        copy.wait()


def weight_swap(weights, jobs, plain, collective_id, after, us):
    n, replicas = lax.axis_size("group"), lax.axis_size("replica")
    piece = weights[0].shape[1] // replicas
    lines = sum(job[1] for job in jobs) + len(plain)
    return pl.pallas_call(
        functools.partial(weight_swap_kernel, n, jobs, len(plain)),
        out_shape=[jax.ShapeDtypeStruct((n, piece, job[1] * job[2]), B16) for job in jobs]
        + [jax.ShapeDtypeStruct(b.shape, b.dtype) for b in plain],
        in_specs=[ANY] * len(jobs) + [VMEM] * len(plain) + [ANY],
        out_specs=[VMEM] * (len(jobs) + len(plain)),
        scratch_shapes=[pltpu.SemaphoreType.DMA((lines, n - 1)) for _ in range(2)]
        + [pltpu.SemaphoreType.DMA((lines,))],
        compiler_params=params(collective_id),
        cost_estimate=cost(us),
        name=f"weight_swap_{collective_id}",
    )(*weights, *plain, after)


def swap(blocks, collective_id, after=None, us=8.0):
    n = lax.axis_size("group")
    count = len(blocks)
    return pl.pallas_call(
        functools.partial(swap_kernel, n, count),
        out_shape=[jax.ShapeDtypeStruct(b.shape, b.dtype) for b in blocks],
        in_specs=[VMEM] * count + [ANY],
        out_specs=[VMEM] * count,
        scratch_shapes=[pltpu.SemaphoreType.DMA((count, n - 1)) for _ in range(2)]
        + [pltpu.SemaphoreType.DMA((count,))],
        compiler_params=params(collective_id),
        cost_estimate=cost(us),
        name=f"swap_{collective_id}",
    )(*blocks, blocks[0] if after is None else after)


def grads_kernel(n, a_ref, b_ref, c_ref, d_ref, *refs):
    o_ref, held, sems = refs[-3:]
    own = held.shape[0]
    cols, width = b_ref.shape[1], d_ref.shape[1]
    folds = c_ref.shape[1] // own
    copies = []
    for i in range(n + folds):
        if i < n:
            lo, size = i * cols, cols
            value = dot_tn(a_ref[:, i * own : (i + 1) * own], b_ref[...])
        else:
            lo, size = n * cols + (i - n) * width, width
            value = dot_tn(c_ref[:, (i - n) * own : (i - n + 1) * own], d_ref[...])
        held[:, lo : lo + size] = value.astype(B16)
        copy = pltpu.make_async_copy(
            held.at[:, pl.ds(lo, size)], o_ref.at[:, pl.ds(lo, size)], sems.at[i]
        )
        copy.start()
        copies.append(copy)
    for copy in copies:
        copy.wait()


def grads_pair(a, b, c, d, after=()):
    n = lax.axis_size("group")
    own = a.shape[1] // n
    folds = c.shape[1] // own
    total = n * b.shape[1] + folds * d.shape[1]
    return pl.pallas_call(
        functools.partial(grads_kernel, n),
        out_shape=jax.ShapeDtypeStruct((own, total), B16),
        in_specs=[VMEM] * 4 + [ANY] * len(after),
        out_specs=pl.BlockSpec(memory_space=pltpu.HBM),
        scratch_shapes=[pltpu.VMEM((own, total), B16), pltpu.SemaphoreType.DMA((n + folds,))],
        compiler_params=pltpu.CompilerParams(vmem_limit_bytes=32 * 1024 * 1024),
        cost_estimate=cost(4.0),
        name="weight_grads",
    )(a, b, c, d, *after)


def digit(value, place):
    return (value // 2**place) % 2


def with_digit(value, place, wanted):
    return value + (wanted - digit(value, place)) * 2**place


def flipped(value, place):
    return value + (1 - 2 * digit(value, place)) * 2**place


def exchange_steps(n, cols, minor, src, o_ref, held, sems, reduce):
    replicas = o_ref.shape[0]
    me = lax.axis_index("group")
    mine = lax.axis_index("replica")
    core = digit(mine, 0)
    spot = mine // 2
    halves = replicas // 2
    bits = halves.bit_length() - 1
    total = o_ref.shape[2]
    flow_cols = total // 2
    orders = (list(range(bits)), list(range(bits))[::-1])
    sibling = flipped(mine, 0)
    peers = [lax.rem(me + step, n) for step in range(1, n)]
    landed = held[0]
    swap_send, swap_recv, out_send, out_recv, side_send, side_recv = sems[:6]

    def to_replica(src_ref, dst_ref, send_sem, recv_sem, target):
        copy = pltpu.make_async_remote_copy(
            src_ref=src_ref,
            dst_ref=dst_ref,
            send_sem=send_sem,
            recv_sem=recv_sem,
            device_id={"replica": target},
            device_id_type=MESH,
        )
        copy.start()
        return copy

    def chosen(order, count, index):
        spot_of = spot
        for i in range(count):
            spot_of = with_digit(spot_of, order[i], (index >> i) % 2)
        return spot_of

    sent = []
    if reduce:
        own_half, first_in, acc, flow_in = held[1:]
        pair_send, pair_recv, flow_send, flow_recv, load_sems = sems[6:]
        loads = []
        for q in range(halves):
            load = pltpu.make_async_copy(src.at[2 * q + core], own_half.at[q], load_sems.at[q])
            load.start()
            loads.append(load)
        paired = []
        for q in range(halves):
            paired.append(
                to_replica(
                    src.at[2 * q + 1 - core], first_in.at[q], pair_send.at[q], pair_recv.at[q], sibling
                )
            )
        sent += paired
        yield
        for q in range(halves):
            loads[q].wait()
            paired[q].wait_recv()
            acc[q] = (own_half[q].astype(F32) + first_in[q].astype(F32)).astype(B16)
        slot = 0
        for stage in range(bits):
            started = []
            for flow in (0, 1):
                lanes = pl.ds(flow * flow_cols, flow_cols)
                place = orders[flow][stage]
                free = orders[flow][stage + 1 :]
                for t in range(2 ** len(free)):
                    keep = chosen(free, len(free), t)
                    copy = to_replica(
                        acc.at[flipped(keep, place), :, lanes],
                        flow_in.at[flow, slot + t],
                        flow_send.at[flow, slot + t],
                        flow_recv.at[flow, slot + t],
                        flipped(mine, place + 1),
                    )
                    started.append((copy, flow, slot + t, keep))
            yield
            for copy, flow, at, keep in started:
                copy.wait_recv()
                lanes = slice(flow * flow_cols, (flow + 1) * flow_cols)
                acc[keep, :, lanes] = (
                    acc[keep, :, lanes].astype(F32) + flow_in[flow, at].astype(F32)
                ).astype(B16)
                sent.append(copy)
            slot += 2 ** (bits - 1 - stage)
        whole = acc.at[spot]
    else:
        whole = src

    swaps = []
    for step, peer in enumerate(peers):
        copy = pltpu.make_async_remote_copy(
            src_ref=whole.at[:, pl.ds(pl.multiple_of(peer * cols, 128), cols)],
            dst_ref=landed.at[me],
            send_sem=swap_send.at[step],
            recv_sem=swap_recv.at[step],
            device_id={"group": peer},
            device_id_type=MESH,
        )
        copy.start()
        swaps.append(copy)
    landed[me] = whole[:, pl.ds(pl.multiple_of(me * cols, 128), cols)]
    o_ref[mine, :, n * cols :] = whole[:, n * cols :]
    yield
    for copy in swaps:
        copy.wait_recv()
    sent += swaps
    inner = cols // minor
    for origin in range(n):
        for m in range(minor):
            lo = (m * n + origin) * inner
            o_ref[mine, :, lo : lo + inner] = landed[origin, :, m * inner : (m + 1) * inner]

    def place_out(spot_of, flow):
        return o_ref.at[2 * spot_of + core, :, pl.ds(flow * flow_cols, flow_cols)]

    sides = []

    def to_side(spot_of, flow, index):
        here = place_out(spot_of, flow)
        sides.append(
            to_replica(here, here, side_send.at[flow, index], side_recv.at[flow, index], sibling)
        )

    slot = 0
    for stage in range(bits):
        started = []
        for flow in (0, 1):
            order = orders[flow][::-1]
            place = order[stage]
            for t in range(2**stage):
                here = place_out(chosen(order, stage, t), flow)
                copy = to_replica(
                    here,
                    here,
                    out_send.at[flow, slot + t],
                    out_recv.at[flow, slot + t],
                    flipped(mine, place + 1),
                )
                started.append((copy, flow, t))
        if stage == 0:
            for flow in (0, 1):
                to_side(spot, flow, 0)
        yield
        for copy, flow, t in started:
            order = orders[flow][::-1]
            copy.wait_recv()
            to_side(flipped(chosen(order, stage, t), order[stage]), flow, 2**stage + t)
            sent.append(copy)
        slot += 2**stage
    yield
    for copy in sides:
        copy.wait_recv()
    for copy in sent + sides:
        copy.wait_send()


def exchange_scratch(n, replicas, piece, total, cols, reduce):
    halves = replicas // 2
    dma = lambda *shape: pltpu.SemaphoreType.DMA(shape)
    held = [pltpu.VMEM((n, piece, cols), B16)]
    sems = [dma(n - 1), dma(n - 1)] + [dma(2, halves) for _ in range(4)]
    if reduce:
        held += [pltpu.VMEM((halves, piece, total), B16) for _ in range(3)]
        held.append(pltpu.VMEM((2, halves - 1, piece, total // 2), B16))
        sems += [dma(halves), dma(halves), dma(2, halves), dma(2, halves), dma(halves)]
    return held + sems


def closing_kernel(n, replicas, layer, attn_cols, ffn_cols, *refs):
    refs = list(refs)

    def take(count):
        some = refs[:count]
        del refs[:count]
        return some

    lhs, raw, xin, gain, res, f_lhs, w_any, f_res, bias, attn_src, ffn_src = take(11)
    take(1)
    g_ref, small_ref, y_ref, attn_out, ffn_out = take(5)
    held, h_sems, w, w_sem = take(4)
    line_b, line_f = take(6), take(6)
    attn_held, attn_sems = take(5), take(11)
    ffn_held, ffn_sems = take(1), take(6)
    me = lax.axis_index("group")
    mine = lax.axis_index("replica")
    rows = res.shape[0]
    bits = (replicas // 2).bit_length() - 1
    others = weight_copies(raw, held, h_sems)
    for other in others:
        other.start()
    w_copy = pltpu.make_async_copy(w_any.at[layer], w, w_sem)
    w_copy.start()
    barrier = pltpu.get_barrier_semaphore()
    for place in range(bits + 1):
        pl.semaphore_signal(
            barrier, inc=1, device_id={"replica": flipped(mine, place)}, device_id_type=MESH
        )
    for step in range(1, n):
        pl.semaphore_signal(
            barrier, inc=1, device_id={"group": lax.rem(me + step, n)}, device_id_type=MESH
        )
    pl.semaphore_wait(barrier, bits + n)

    attn = exchange_steps(n, attn_cols, 3, attn_src, attn_out, attn_held, attn_sems, True)
    ffn = exchange_steps(n, ffn_cols, 1, ffn_src, ffn_out, ffn_held, ffn_sems, False)
    next(attn)
    for other in others:
        other.wait()

    def part(block, into):
        own = lhs[rows_at(block, rows), :]
        for chunk in range(CH):
            into[chunk] = dot_nt(own, weight_rows(held, chunk))

    def early(step):
        if step == 0:
            next(attn, None)
            next(ffn, None)
        else:
            next(ffn, None)
        if step == n - 2:
            next(attn, None)

    line_scatter(n, me, part, *line_b, hook=early)
    grad = joined(line_b[3])
    _, normed, inverse = norm_apply(xin[...], gain[...], gain[...])
    result = res[...] + norm_back(grad, normed, inverse, gain[...])
    g_ref[...] = result
    small_ref[0:1, :] = jnp.sum(grad * normed, axis=0, keepdims=True)
    small_ref[1:2, :] = jnp.sum(grad, axis=0, keepdims=True)
    small_ref[2:3, :] = jnp.sum(result, axis=0, keepdims=True)
    next(attn, None)
    w_copy.wait()
    cols = w.shape[1] // CH

    def f_part(block, into):
        own = f_lhs[rows_at(block, rows), :]
        for chunk in range(CH):
            into[chunk] = dot(own, w[:, chunk * cols : (chunk + 1) * cols])

    def late(step):
        next(attn, None)
        if step:
            next(ffn, None)

    line_scatter(n, me, f_part, *line_f, hook=late)
    y_ref[...] = f_res[...] + joined(line_f[3]) + bias[...]
    for steps in (attn, ffn):
        for _ in steps:
            pass


def closing_step(lhs, raw, xin, gain, res, f_lhs, w_all, layer, f_res, bias, attn_grads, ffn_mine, attn_cols, ffn_cols, after):
    n, replicas = lax.axis_size("group"), lax.axis_size("replica")
    rows, width = res.shape
    own, attn_total = attn_grads.shape
    piece, ffn_total = ffn_mine.shape
    full = lambda total: jax.ShapeDtypeStruct((replicas, piece, total), B16)
    flat = jax.ShapeDtypeStruct((rows, width), F32)
    outs = pl.pallas_call(
        functools.partial(closing_kernel, n, replicas, layer, attn_cols, ffn_cols),
        out_shape=[flat, jax.ShapeDtypeStruct((8, width), F32), flat, full(attn_total), full(ffn_total)],
        in_specs=[VMEM, ANY, VMEM, VMEM, VMEM, VMEM, ANY, VMEM, VMEM, ANY, VMEM, ANY],
        out_specs=[VMEM] * 5,
        scratch_shapes=weight_scratch(raw)
        + [pltpu.VMEM(w_all.shape[1:], B16), pltpu.SemaphoreType.DMA]
        + scatter_scratch(n, rows, width)
        + scatter_scratch(n, rows, width)
        + exchange_scratch(n, replicas, piece, attn_total, attn_cols, True)
        + exchange_scratch(n, replicas, piece, ffn_total, ffn_cols, False),
        compiler_params=params(70),
        cost_estimate=cost(50.0),
        name="closing",
    )(
        lhs, raw, xin, gain, res, f_lhs, w_all, f_res, bias,
        attn_grads.reshape(replicas, piece, attn_total), ffn_mine, after,
    )
    g, small, y, attn_full, ffn_full = outs
    return g, small, y, attn_full.reshape(own, attn_total), ffn_full.reshape(own, ffn_total)


def small_sums_kernel(n, replicas, wide, ups, o_ref, landed, both, spread, *sems):
    a_send, a_recv, b_send, b_recv = sems
    me = lax.axis_index("group")
    mine = lax.axis_index("replica")
    rows = landed.shape[1]
    peers = [lax.rem(me + step, n) for step in range(1, n)]
    mates = [lax.rem(mine + step, replicas) for step in range(1, replicas)]
    barrier = pltpu.get_barrier_semaphore()
    for peer in peers:
        pl.semaphore_signal(barrier, inc=1, device_id={"group": peer}, device_id_type=MESH)
    for mate in mates:
        pl.semaphore_signal(barrier, inc=1, device_id={"replica": mate}, device_id_type=MESH)
    pl.semaphore_wait(barrier, n + replicas - 2)
    copies = []
    for step, peer in enumerate(peers):
        copy = pltpu.make_async_remote_copy(
            src_ref=wide.at[peer],
            dst_ref=landed.at[me],
            send_sem=a_send.at[step],
            recv_sem=a_recv.at[step],
            device_id={"group": peer},
            device_id_type=MESH,
        )
        copy.start()
        copies.append(copy)
    landed[me] = wide[me]
    for copy in copies:
        copy.wait_recv()
    total = landed[0]
    for i in range(1, n):
        total = total + landed[i]
    both[0:rows, :] = total
    both[rows:, :] = ups[...]
    spread[mine] = both[...]
    others = []
    for step, mate in enumerate(mates):
        copy = pltpu.make_async_remote_copy(
            src_ref=both,
            dst_ref=spread.at[mine],
            send_sem=b_send.at[step],
            recv_sem=b_recv.at[step],
            device_id={"replica": mate},
            device_id_type=MESH,
        )
        copy.start()
        others.append(copy)
    for copy in others:
        copy.wait_recv()
    total = spread[0]
    for i in range(1, replicas):
        total = total + spread[i]
    o_ref[...] = total
    for copy in copies + others:
        copy.wait_send()


def small_sums(wide, ups, collective_id):
    n, replicas = lax.axis_size("group"), lax.axis_size("replica")
    _, rows, own = wide.shape
    lines = rows + ups.shape[0]
    return pl.pallas_call(
        functools.partial(small_sums_kernel, n, replicas),
        out_shape=jax.ShapeDtypeStruct((lines, own), F32),
        in_specs=[VMEM, VMEM],
        out_specs=VMEM,
        scratch_shapes=[
            pltpu.VMEM((n, rows, own), F32),
            pltpu.VMEM((lines, own), F32),
            pltpu.VMEM((replicas, lines, own), F32),
            pltpu.SemaphoreType.DMA((n - 1,)),
            pltpu.SemaphoreType.DMA((n - 1,)),
            pltpu.SemaphoreType.DMA((replicas - 1,)),
            pltpu.SemaphoreType.DMA((replicas - 1,)),
        ],
        compiler_params=params(collective_id),
        cost_estimate=cost(9.0),
        name="small_sums",
    )(wide, ups)


def widen_kernel(lead, *refs):
    full, cols_out, rows_out = refs[0], refs[-2], refs[-1]
    step = pl.program_id(0)

    @pl.when(step < lead)
    def _():
        cols_out[0] = full[...].astype(F32)

    @pl.when(step >= lead)
    def _():
        rows_out[0] = full[...].astype(F32)


def widen(full, cut, width, layer, layers, before):
    own, total = full.shape
    lead, folds = cut // width, (total - cut) // width
    block = (1, own, width)
    return pl.pallas_call(
        functools.partial(widen_kernel, lead),
        grid=(lead + folds,),
        out_shape=[
            jax.ShapeDtypeStruct((layers, own, cut), F32),
            jax.ShapeDtypeStruct((layers, own * folds, width), F32),
        ],
        in_specs=[pl.BlockSpec((own, width), lambda j: (0, j))] + [ANY] * len(before),
        out_specs=[
            pl.BlockSpec(block, lambda j: (layer, 0, jnp.minimum(j, lead - 1))),
            pl.BlockSpec(block, lambda j: (layer, jnp.maximum(j - lead, 0), 0)),
        ],
        input_output_aliases={1: 0, 2: 1} if before else {},
        compiler_params=pltpu.CompilerParams(vmem_limit_bytes=24 * 1024 * 1024),
        cost_estimate=cost(own * total * 6 / 3.3e6),
        name=f"widen_{layer}",
    )(full, *before)


def attention(q, k, v, first_head, heads_here):
    tokens = q.shape[0]
    split = lambda m: m.reshape(tokens, heads_here, HEAD_DIM).transpose(1, 0, 2)
    q, k, v = split(q), split(k), split(v)
    head_ids = (first_head + jnp.arange(heads_here, dtype=jnp.int32)).astype(F32)
    slopes = 2.0 ** (-8.0 * (head_ids + 1.0) / HEADS)
    pos = jnp.arange(tokens, dtype=jnp.int32)
    offset = (pos[:, None] - pos[None, :]).astype(F32)
    raw = jnp.einsum("hqd,hkd->hqk", q, k, preferred_element_type=F32)
    scores = raw * HEAD_DIM ** (-0.5) - slopes[:, None, None] * offset[None]
    scores = jnp.where((offset >= 0.0)[None], scores, NEG)
    row_top = jnp.max(scores, axis=-1, keepdims=True)
    exps_raw = jnp.exp(scores - row_top)
    row_total = jnp.sum(exps_raw, axis=-1, keepdims=True)
    probs = (exps_raw * (1.0 / row_total)).astype(B16)
    context = jnp.einsum("hqk,hkd->hqd", probs, v, preferred_element_type=F32).astype(B16)
    return context.transpose(1, 0, 2).reshape(tokens, -1), (q, k, v, probs, context)


def attention_back(d_context, saved):
    q, k, v, probs, context = saved
    heads_here, tokens, _ = q.shape
    dc = d_context.reshape(tokens, heads_here, HEAD_DIM).transpose(1, 0, 2)
    d_probs = jnp.einsum("hqd,hkd->hqk", dc, v, preferred_element_type=F32)
    delta = jnp.sum(dc.astype(F32) * context.astype(F32), axis=-1, keepdims=True)
    ds = (probs.astype(F32) * (d_probs - delta)).astype(B16)
    scale = HEAD_DIM ** (-0.5)
    dq = jnp.einsum("hqk,hkd->hqd", ds, k, preferred_element_type=F32) * scale
    dk = jnp.einsum("hqk,hqd->hkd", ds, q, preferred_element_type=F32) * scale
    dv = jnp.einsum("hqk,hqd->hkd", probs, dc, preferred_element_type=F32)
    sums = (jnp.sum(dq, axis=1).reshape(-1), jnp.sum(dv, axis=1).reshape(-1))
    join = lambda m: m.astype(B16).transpose(1, 0, 2).reshape(tokens, -1)
    return jnp.concatenate([join(dq), join(dk), join(dv)], axis=1), sums


def local(
    inputs,
    cotangent,
    norm_gain,
    norm_bias,
    w_qkv,
    bias_qv,
    w_out,
    bias_out,
    w_up,
    bias_up,
    w_down,
    bias_down,
):
    groups = lax.axis_size("group")
    replicas = lax.axis_size("replica")
    me = lax.axis_index("group")
    copy_idx = lax.axis_index("replica")
    layers, own, _ = w_qkv.shape
    width = own * groups
    ff_own = w_down.shape[1]
    heads_here = HEADS // groups
    piece = own // replicas

    def share(block):
        full = lax.all_gather(block, "replica", axis=0)
        if piece % 16:
            full = full.transpose(1, 0, 2, 3).reshape(1, 1, width, -1)
        return full

    small = jnp.concatenate(
        [norm_gain, norm_bias, bias_qv.reshape(layers, 2, own), bias_out[:, None], bias_down[:, None]],
        axis=1,
    ).reshape(layers * 8, own)
    small = jnp.broadcast_to(small[None], (groups,) + small.shape)
    wq_first, small = weight_swap([w_qkv], [(0, 3, own)], [small], 0, bias_up, 9.0)
    wq = [share(wq_first)] + [None] * (layers - 1)
    wu = [None] * layers

    small = small.reshape(groups, layers, 8, own).astype(F32)
    rows_of = lambda i: small[:, :, i].transpose(1, 0, 2).reshape(layers, width)
    gains = [rows_of(0), rows_of(1)]
    shifts = [rows_of(2), rows_of(3)]
    qv_full = small[:, :, 4:6].transpose(1, 0, 2, 3).reshape(layers, 2 * width)
    q_bias = lax.dynamic_slice_in_dim(qv_full, me * own, own, axis=1)
    v_bias = lax.dynamic_slice_in_dim(qv_full, width + me * own, own, axis=1)
    qkv_bias = jnp.concatenate([q_bias, jnp.zeros_like(q_bias), v_bias], axis=1)
    out_bias, down_bias = rows_of(6), rows_of(7)
    up_bias = bias_up.astype(F32)

    x = inputs[0].astype(F32)
    vec0 = jnp.stack([gains[0][0], shifts[0][0]])
    a1_all = first_gather(inputs[0], vec0, 1, True, wq_first)
    jobs = [(l, 1, ff_own) for l in range(layers)] + [(l, 3, own) for l in range(1, layers)]
    later = weight_swap([w_up] * layers + [w_qkv] * (layers - 1), jobs, [], 2, a1_all, 18.0)
    for l in range(layers):
        wu[l] = share(later[l])
        if l:
            wq[l] = share(later[layers + l - 1])
    cot_all = first_gather(cotangent[0], vec0, 3, False, later[0])

    full0 = wq[0].transpose(1, 0, 2, 3).reshape(width, 3 * own)
    proj = (dot(a1_all, full0) + qkv_bias[0]).astype(B16)
    kept = []
    for l in range(layers):
        cut = lambda i: proj[:, i * own : (i + 1) * own]
        context, attn_saved = attention(cut(0), cut(1), cut(2), me * heads_here, heads_here)
        vec = jnp.stack([out_bias[l], gains[1][l], shifts[1][l]])
        h, a2_all, hidden, slope = forward_step(
            context, w_out, l, x, vec, 10 + 4 * l, "gelu", wu[l], up_bias[l][None]
        )
        saved = (x, a1_all, attn_saved, context, h, a2_all, slope, hidden)
        if l + 1 < layers:
            vec = jnp.stack([down_bias[l], gains[0][l + 1], shifts[0][l + 1]])
            x, a1_all, proj = forward_step(
                hidden, w_down, l, h, vec, 11 + 4 * l, "bias", wq[l + 1], qkv_bias[l + 1][None]
            )
        kept.append(saved)

    def reduce_pair(grads):
        return lax.psum_scatter(grads, "replica", scatter_dimension=0, tiled=True)

    def swap_pair(mine, cols, collective_id, after=None):
        cut = groups * cols
        left = mine[:, :cut].reshape(piece, groups, cols).transpose(1, 0, 2)
        return swap([left], collective_id, after)[0]

    def share_pair(left, mine, cols, minor):
        cut = groups * cols
        left = left.reshape(groups, piece, minor, cols // minor).transpose(1, 2, 0, 3)
        mine = jnp.concatenate([left.reshape(piece, cut), mine[:, cut:]], axis=1)
        return lax.all_gather(mine, "replica", axis=0, tiled=True)

    g = cotangent[0].astype(F32)
    g_sum = jnp.sum(g, axis=0)
    g_all = cot_all
    smalls = [None] * layers
    ffn_sum = [None] * layers
    attn_sum = [None] * layers
    ffn_full = [None] * layers
    attn_full = [None] * layers
    zeros_qv = jnp.zeros((2 * width,), F32)
    pre = up_sum = None
    waits = ()
    for l in reversed(range(layers)):
        x_in, a1_all, attn_saved, context, h, a2_all, slope, hidden = kept[l]
        if pre is None:
            d_pre = dot_nt(g_all, w_down[l]) * slope
            up_sum = jnp.sum(d_pre, axis=0)
            pre = d_pre.astype(B16)
        ffn_grads = grads_pair(a2_all, pre, hidden, g_all)
        ffn_sum[l] = reduce_pair(ffn_grads)
        down_sum, ups = g_sum, up_sum
        dh, small1, dh_all, dc = backward_step(
            pre, wu[l], h, gains[1][l][None], g, 30 + 4 * l, "plain", w_out, l, after=(ffn_grads,) + waits
        )
        d_proj, (dq_sum, dv_sum) = attention_back(dc, attn_saved)
        attn_grads = grads_pair(a1_all, d_proj, context, dh_all, (ffn_sum[l],) if l else ())
        if l:
            attn_sum[l] = reduce_pair(attn_grads)
            ffn_left = swap_pair(ffn_sum[l], ff_own, 60 + 4 * l, attn_grads)
            ffn_full[l] = share_pair(ffn_left, ffn_sum[l], ff_own, 1)
            g, small0, g_all, pre, up_sum = backward_step(
                d_proj, wq[l], x_in, gains[0][l][None], dh, 31 + 4 * l, "gelu", w_down, l - 1, kept[l - 1][6],
                after=(attn_grads, ffn_left),
            )
            attn_left = swap_pair(attn_sum[l], 3 * own, 61 + 4 * l, small0)
            attn_full[l] = share_pair(attn_left, attn_sum[l], 3 * own, 3)
            waits = (attn_left,)
            g_sum, up_sum = small0[2], up_sum[0]
        else:
            last = kept[layers - 1]
            g, small0, x, attn_full[l], ffn_full[l] = closing_step(
                d_proj, wq[l], x_in, gains[0][l][None], dh, last[7], w_down, layers - 1, last[4],
                down_bias[layers - 1][None], attn_grads, ffn_sum[l], 3 * own, ff_own, attn_grads,
            )
            outputs = x.astype(B16)[None]
        qv = lax.dynamic_update_slice_in_dim(zeros_qv, dq_sum, me * own, axis=0)
        qv = lax.dynamic_update_slice_in_dim(qv, dv_sum, width + me * own, axis=0)
        smalls[l] = (
            jnp.concatenate([small0[0], small1[0], small0[1], small1[1], qv, small1[2], down_sum]),
            ups,
        )

    ffn_out, attn_out = (), ()
    for l in reversed(range(layers)):
        ffn_out = tuple(widen(ffn_full[l], groups * ff_own, width, l, layers, ffn_out))
        attn_out = tuple(widen(attn_full[l], 3 * width, width, l, layers, attn_out))

    wide = jnp.stack([s[0] for s in smalls])
    per_owner = lambda lo, n: wide[:, lo * width : (lo + n) * width].reshape(layers, n, groups, own)
    gain_bias = per_owner(0, 4).transpose(2, 0, 1, 3)
    qv = wide[:, 4 * width : 6 * width].reshape(layers, groups, 2, own).transpose(1, 0, 2, 3)
    dense = per_owner(6, 2).transpose(2, 0, 1, 3)
    wide = jnp.concatenate([gain_bias, qv, dense], axis=2)
    ups = jnp.stack([s[1] for s in smalls]).reshape(-1, own)
    total = small_sums(wide.reshape(groups, layers * 8, own), ups, 5)
    own_cols = total[: layers * 8].reshape(layers, 8, own)
    up_total = total[layers * 8 :].reshape(layers, ff_own)
    qv_total = own_cols[:, 4:6].reshape(layers, 2 * own)
    return (
        outputs,
        g[None],
        own_cols[:, 0:2],
        own_cols[:, 2:4],
        attn_out[0],
        qv_total,
        attn_out[1],
        own_cols[:, 6],
        ffn_out[0],
        up_total,
        ffn_out[1],
        own_cols[:, 7],
    )


def solution(mesh):
    rows = P("replica", "group", None)
    vec = P(None, None, "group")
    mat = P(None, "group", None)
    bias = P(None, "group")
    params_in = (vec, vec, mat, bias, mat, bias, mat, bias, mat, bias)
    return jax.shard_map(
        local,
        mesh=mesh,
        in_specs=(rows, rows) + params_in,
        out_specs=(rows, rows) + params_in,
        check_vma=False,
    )
```
